32 devices in a mesh: shard: 8 (over z, x), ctx: 4 (over y, core).
Axes of the slice: x: 2, y: 2, z: 4, core: 2. Of those that a mesh axis runs over, the one named last changes fastest.
Arguments:
- layer_input: bfloat16 [16, 256, 640], P('shard', 'ctx'), may hold values from -4 to 4
- out_cotangent: bfloat16 [16, 256, 640], P('shard', 'ctx'), may hold values from -6 to 6
- block_pairs: int32 [16, 4], P('shard'), may hold values from 0 to 3, each once within a row
- w_query: bfloat16 [640, 1024], P(None, 'shard'), may hold values from -0.0625 to 0.0625
- w_key: bfloat16 [640, 256], P(None, 'shard'), may hold values from -0.0625 to 0.0625
- w_value: bfloat16 [640, 256], P(None, 'shard'), may hold values from -0.25 to 0.25
- w_output: bfloat16 [1024, 640], P('shard'), may hold values from -0.1875 to 0.1875
- w_gate: bfloat16 [640, 2048], P(None, 'shard'), may hold values from -0.25 to 0.25
- w_up: bfloat16 [640, 2048], P(None, 'shard'), may hold values from -0.25 to 0.25
- w_down: bfloat16 [2048, 640], P('shard'), may hold values from -0.125 to 0.125
- input_gain: bfloat16 [640], P('shard'), may hold values from 0.099609375 to 1.8984375
- attnpost_gain: bfloat16 [640], P('shard'), may hold values from 0.099609375 to 1.8984375
- ffnpre_gain: bfloat16 [640], P('shard'), may hold values from 0.099609375 to 1.8984375
- ffnpost_gain: bfloat16 [640], P('shard'), may hold values from 0.099609375 to 1.8984375
- query_gain: bfloat16 [256], P('shard'), may hold values from 0.5 to 3
- key_gain: bfloat16 [256], P('shard'), may hold values from 0.5 to 3
Outputs:
- layer_output: bfloat16 [16, 256, 640], P('shard', 'ctx')
- input_grad: float32 [16, 256, 640], P('shard', 'ctx')
- wgrad_query: float32 [640, 1024], P(None, 'shard')
- wgrad_key: float32 [640, 256], P(None, 'shard')
- wgrad_value: float32 [640, 256], P(None, 'shard')
- wgrad_output: float32 [1024, 640], P('shard')
- wgrad_gate: float32 [640, 2048], P(None, 'shard')
- wgrad_up: float32 [640, 2048], P(None, 'shard')
- wgrad_down: float32 [2048, 640], P('shard')
- ggrad_input: float32 [640], P('shard')
- ggrad_attnpost: float32 [640], P('shard')
- ggrad_ffnpre: float32 [640], P('shard')
- ggrad_ffnpost: float32 [640], P('shard')
- ggrad_query: float32 [256], P('shard')
- ggrad_key: float32 [256], P('shard')
The draws below stay inside these ranges and needn't reach their ends.
Inputs may be any that keep to these rules, and one draw needn't show every extreme that they name: Each row names every block pair once; context rank c holds blocks block_pairs[s, c] and 7 - block_pairs[s, c] of sequence s, in that order.
All inputs are finite; a program needn't handle non-finite values.
Results may differ from the reference program's by a relative error of at most 0.025.
The reference program's roundings to bfloat16 on the way count: a program that leaves them out, or rounds other values in their place, can miss the bound.
Values may be sent and summed in bfloat16 or wider, within the bound.
No kernel may reach another device: no remote copies, remote signals or barrier semaphores. Data moves between devices by JAX's collectives and lax.ppermute only.
A program may use at most 128 MiB of HBM per device.

```python
import math
import jax
import jax.numpy as jnp
from jax import lax

D = 640
H = 4
HD = 256
FF = 2048
BLK = 32
HQ = 1024
SEQS = 16
L = 256
N_CTX = 4


weight_edge = 0.0625


def uniform_block(key, tag, rows, columns):
    return jax.random.uniform(jax.random.fold_in(key, tag), (rows, columns), jnp.float32, -weight_edge, weight_edge)


def draw_layer_input(key, part):
    base = jnp.clip(jax.random.normal(jax.random.fold_in(key, 7321), (SEQS, L, D), jnp.float32), -4.0, 4.0)
    return base.astype(jnp.bfloat16)


def draw_w_query(key, part):
    return uniform_block(key, 7305, D, HQ).astype(jnp.bfloat16)


def draw_w_key(key, part):
    return uniform_block(key, 7307, D, HD).astype(jnp.bfloat16)


def gain_values(key, tag):
    exponent = jax.random.uniform(jax.random.fold_in(key, tag + 1), (HD,), jnp.float32, math.log(0.5), math.log(3.0))
    return jnp.clip(jnp.exp(exponent), 0.5, 3.0)


def draw_query_gain(key, part):
    return gain_values(key, 7311).astype(jnp.bfloat16)


def draw_key_gain(key, part):
    return gain_values(key, 7313).astype(jnp.bfloat16)


def level_of(key, dims, shards, least, largest):
    loudness = 1.0
    for axis_at, blocks in shards:
        heights = jax.random.uniform(jax.random.fold_in(jax.random.fold_in(key, 6), axis_at), (blocks,), jnp.float32, least / len(shards), largest / len(shards))
        loudness = loudness * jnp.repeat(jnp.exp(heights), dims[axis_at] // blocks).reshape((-1,) + (1,) * (len(dims) - 1 - axis_at))
    return loudness


def scatter_about(key, extent, spread, reach, split=(), kind=jnp.bfloat16):
    array = jax.random.normal(key, extent, jnp.float32) * spread
    if len(split) > 0:
        array = level_of(key, extent, split, -0.22, 0.18) * array
    return jnp.clip(array, min=-reach, max=reach).astype(kind)


def setup_inputs(seed: int = 0) -> dict:
    streams_of = jax.random.split(jax.random.key(seed), 17)
    return {
        "layer_input": draw_layer_input(jax.random.fold_in(streams_of[16], 71), 0),
        "out_cotangent": scatter_about(streams_of[1], (SEQS, L, D), 1.0, 6.0, ((0, 8), (1, 4))),
        "block_pairs": jax.vmap(lambda own: jax.random.permutation(own, N_CTX))(jax.random.split(streams_of[2], SEQS)).reshape((SEQS, N_CTX)).astype(jnp.int32),
        "w_query": draw_w_query(jax.random.fold_in(streams_of[16], 71), 0),
        "w_key": draw_w_key(jax.random.fold_in(streams_of[16], 71), 0),
        "w_value": scatter_about(streams_of[5], (D, HD), D ** -0.5, 0.25, ((1, 8),)),
        "w_output": scatter_about(streams_of[6], (HQ, D), HQ ** -0.5, 0.1875, ((0, 8),)),
        "w_gate": scatter_about(streams_of[7], (D, FF), D ** -0.5, 0.25, ((1, 8),)),
        "w_up": scatter_about(streams_of[8], (D, FF), D ** -0.5, 0.25, ((1, 8),)),
        "w_down": scatter_about(streams_of[9], (FF, D), FF ** -0.5, 0.125, ((0, 8),)),
        "input_gain": jnp.clip(1.0 + 0.18 * jax.random.normal(streams_of[10], (D,), jnp.float32), 0.099609375, 1.8984375).astype(jnp.bfloat16),
        "attnpost_gain": jnp.clip(1.0 + 0.18 * jax.random.normal(streams_of[11], (D,), jnp.float32), 0.099609375, 1.8984375).astype(jnp.bfloat16),
        "ffnpre_gain": jnp.clip(1.0 + 0.18 * jax.random.normal(streams_of[12], (D,), jnp.float32), 0.099609375, 1.8984375).astype(jnp.bfloat16),
        "ffnpost_gain": jnp.clip(1.0 + 0.18 * jax.random.normal(streams_of[13], (D,), jnp.float32), 0.099609375, 1.8984375).astype(jnp.bfloat16),
        "query_gain": draw_query_gain(jax.random.fold_in(streams_of[16], 71), 0),
        "key_gain": draw_key_gain(jax.random.fold_in(streams_of[16], 71), 0),
    }


epsilon = 1e-06
rope_base = 1000000.0

def norm_rows(vector, scaling):
    mean_sq = lax.optimization_barrier(jnp.mean(vector * vector, axis=-1, keepdims=True))
    return vector * lax.rsqrt(mean_sq + epsilon) * scaling

def rope_tables(positions, width):
    half = width // 2
    index = jnp.arange(half).astype(jnp.float32)
    freq = jnp.power(rope_base, -(2.0 * index) / width)
    angle = positions.astype(jnp.float32)[..., None] * freq
    return (jnp.cos(angle), jnp.sin(angle))

def rotate(vector, cosine, sine):
    half = vector.shape[-1] // 2
    first = vector[..., :half]
    second = vector[..., half:]
    return jnp.concatenate([first * cosine - second * sine, second * cosine + first * sine], axis=-1)

def head_prep(raw, scaling, cosine, sine):
    return rotate(norm_rows(raw, scaling), cosine, sine)

def gated_unit(gate, upward):
    return jax.nn.gelu(gate, approximate=True) * upward

def seq_positions(pairs, blk):
    count = pairs.shape[-1]
    offset = jnp.arange(2 * blk, dtype=jnp.int32)
    chosen = pairs[..., None].astype(jnp.int32)
    block = jnp.where(offset < blk, chosen, 2 * count - 1 - chosen)
    places = block * blk + offset % blk
    return places.reshape(pairs.shape[:-1] + (count * 2 * blk,))

def reference(layer_input, out_cotangent, block_pairs, w_query, w_key, w_value, w_output, w_gate, w_up, w_down, input_gain, attnpost_gain, ffnpre_gain, ffnpost_gain, query_gain, key_gain):
    bf = jnp.bfloat16
    f32 = jnp.float32
    g_in = input_gain.astype(f32)
    g_pa = attnpost_gain.astype(f32)
    g_pf = ffnpre_gain.astype(f32)
    g_po = ffnpost_gain.astype(f32)
    g_q = query_gain.astype(f32)
    g_k = key_gain.astype(f32)
    scale = 1.0 / 16.0

    def one_sequence(carry, inputs):
        seq_in, seq_cot, pairs = inputs
        positions = seq_positions(pairs, BLK)
        length = seq_in.shape[0]
        x_f = seq_in.astype(f32)
        normed_in = norm_rows(x_f, g_in).astype(bf)
        query_raw = jnp.dot(normed_in, w_query, preferred_element_type=f32).reshape(length, H, HD)
        key_raw = jnp.dot(normed_in, w_key, preferred_element_type=f32)
        values = jnp.dot(normed_in, w_value, preferred_element_type=f32).astype(bf)
        cosine, sine = rope_tables(positions, HD)
        q_cos = cosine[:, None, :]
        q_sin = sine[:, None, :]
        query_rot = head_prep(query_raw, g_q, q_cos, q_sin).astype(bf)
        key_rot = head_prep(key_raw, g_k, cosine, sine).astype(bf)
        mask = positions[None, :] <= positions[:, None]
        scores = jnp.einsum('qhd,kd->hqk', query_rot.astype(f32), key_rot.astype(f32)) * scale
        scores = jnp.where(mask[None], scores, -1e+30)
        top = lax.optimization_barrier(jnp.max(scores, axis=-1, keepdims=True))
        lse = top + jnp.log(lax.optimization_barrier(jnp.sum(jnp.exp(scores - top), axis=-1, keepdims=True)))
        probs32 = jnp.exp(scores - lse)
        probs = probs32.astype(bf)
        attended = jnp.einsum('hqk,kd->qhd', probs.astype(f32), values.astype(f32)).reshape(length, HQ).astype(bf)
        projected = jnp.dot(attended, w_output, preferred_element_type=f32)
        resid = x_f + norm_rows(projected, g_pa)
        normed_mid = norm_rows(resid, g_pf).astype(bf)
        gate = jnp.dot(normed_mid, w_gate, preferred_element_type=f32)
        upward = jnp.dot(normed_mid, w_up, preferred_element_type=f32)
        hidden = gated_unit(gate, upward).astype(bf)
        ffn_out = jnp.dot(hidden, w_down, preferred_element_type=f32)
        seq_out = (resid + norm_rows(ffn_out, g_po)).astype(bf)
        cot = seq_cot.astype(f32)
        unused, pull = jax.vjp(norm_rows, ffn_out, g_po)
        d_ffn, dg_po = pull(cot)
        d_ffn_b = d_ffn.astype(bf)
        gw_down = jnp.dot(hidden.T, d_ffn_b, preferred_element_type=f32)
        d_hidden = jnp.dot(d_ffn_b, w_down.T, preferred_element_type=f32)
        unused, pull = jax.vjp(gated_unit, gate, upward)
        d_gate, d_upward = pull(d_hidden)
        d_gate = d_gate.astype(bf)
        d_upward = d_upward.astype(bf)
        gw_gate = jnp.dot(normed_mid.T, d_gate, preferred_element_type=f32)
        gw_up = jnp.dot(normed_mid.T, d_upward, preferred_element_type=f32)
        d_mid = jnp.dot(d_gate, w_gate.T, preferred_element_type=f32) + jnp.dot(d_upward, w_up.T, preferred_element_type=f32)
        unused, pull = jax.vjp(norm_rows, resid, g_pf)
        d_resid_n, dg_pf = pull(d_mid)
        d_resid = cot + d_resid_n
        unused, pull = jax.vjp(norm_rows, projected, g_pa)
        d_projected, dg_pa = pull(d_resid)
        d_proj_b = d_projected.astype(bf)
        gw_output = jnp.dot(attended.T, d_proj_b, preferred_element_type=f32)
        d_attended = jnp.dot(d_proj_b, w_output.T, preferred_element_type=f32).astype(bf).reshape(length, H, HD)
        d_probs = jnp.einsum('qhd,kd->hqk', d_attended.astype(f32), values.astype(f32))
        delta = lax.optimization_barrier(jnp.sum(probs32 * d_probs, axis=-1, keepdims=True))
        d_scores = (probs32 * (d_probs - delta) * scale).astype(bf)
        d_query_rot = jnp.einsum('hqk,kd->qhd', d_scores.astype(f32), key_rot.astype(f32))
        d_key_rot = jnp.einsum('hqk,qhd->kd', d_scores.astype(f32), query_rot.astype(f32))
        d_values = jnp.einsum('hqk,qhd->kd', probs.astype(f32), d_attended.astype(f32)).astype(bf)
        unused, pull = jax.vjp(lambda raw, scaling: head_prep(raw, scaling, q_cos, q_sin), query_raw, g_q)
        d_query, dg_q = pull(d_query_rot)
        unused, pull = jax.vjp(lambda raw, scaling: head_prep(raw, scaling, cosine, sine), key_raw, g_k)
        d_key, dg_k = pull(d_key_rot)
        d_query = d_query.astype(bf).reshape(length, HQ)
        d_key = d_key.astype(bf)
        gw_query = jnp.dot(normed_in.T, d_query, preferred_element_type=f32)
        gw_key = jnp.dot(normed_in.T, d_key, preferred_element_type=f32)
        gw_value = jnp.dot(normed_in.T, d_values, preferred_element_type=f32)
        d_in = jnp.dot(d_query, w_query.T, preferred_element_type=f32) + jnp.dot(d_key, w_key.T, preferred_element_type=f32) + jnp.dot(d_values, w_value.T, preferred_element_type=f32)
        unused, pull = jax.vjp(norm_rows, x_f, g_in)
        d_x_n, dg_in = pull(d_in)
        seq_grad = d_resid + d_x_n
        terms = (gw_query, gw_key, gw_value, gw_output, gw_gate, gw_up, gw_down, dg_in, dg_pa, dg_pf, dg_po, dg_q, dg_k)
        carry = tuple((total + term for total, term in zip(carry, terms)))
        return (carry, (seq_out, seq_grad))
    start = (jnp.zeros((D, HQ), jnp.float32), jnp.zeros((D, HD), jnp.float32), jnp.zeros((D, HD), jnp.float32), jnp.zeros((HQ, D), jnp.float32), jnp.zeros((D, FF), jnp.float32), jnp.zeros((D, FF), jnp.float32), jnp.zeros((FF, D), jnp.float32), jnp.zeros((D,), jnp.float32), jnp.zeros((D,), jnp.float32), jnp.zeros((D,), jnp.float32), jnp.zeros((D,), jnp.float32), jnp.zeros((HD,), jnp.float32), jnp.zeros((HD,), jnp.float32))
    totals, stacked = lax.scan(one_sequence, start, (layer_input, out_cotangent, block_pairs))
    layer_output, input_grad = stacked
    return (layer_output, input_grad, totals[0], totals[1], totals[2], totals[3], totals[4], totals[5], totals[6], totals[7], totals[8], totals[9], totals[10], totals[11], totals[12])
```

```python
import functools

import jax
import jax.numpy as jnp
from jax import lax
from jax.experimental import pallas as pl
from jax.experimental.pallas import tpu as pltpu
from jax.sharding import PartitionSpec as P

epsilon = 1e-06
rope_base = 1000000.0
bf = jnp.bfloat16
f32 = jnp.float32


def norm_rows(vector, scaling):
    mean_sq = jnp.mean(vector * vector, axis=-1, keepdims=True)
    return vector * lax.rsqrt(mean_sq + epsilon) * scaling


def rope_tables(positions, width):
    half = width // 2
    index = jnp.arange(half).astype(jnp.float32)
    freq = jnp.power(rope_base, -(2.0 * index) / width)
    angle = positions.astype(jnp.float32)[..., None] * freq
    return (jnp.cos(angle), jnp.sin(angle))


def rotate(vector, cosine, sine):
    half = vector.shape[-1] // 2
    first = vector[..., :half]
    second = vector[..., half:]
    return jnp.concatenate(
        [first * cosine - second * sine, second * cosine + first * sine], axis=-1
    )


def head_prep(raw, scaling, cosine, sine):
    return rotate(norm_rows(raw, scaling), cosine, sine)


def gated_unit(gate, upward):
    return jax.nn.gelu(gate, approximate=True) * upward


def seq_positions(pairs, blk):
    count = pairs.shape[-1]
    offset = jnp.arange(2 * blk, dtype=jnp.int32)
    chosen = pairs[..., None]
    block = jnp.where(offset < blk, chosen, 2 * count - 1 - chosen)
    places = block * blk + offset % blk
    return places.reshape(pairs.shape[:-1] + (count * 2 * blk,))


class Axis:
    def __init__(self, name):
        self.name = name
        self.size = lax.axis_size(name)
        self.inner = 2 if self.size % 2 == 0 else 1
        self.outer = self.size // self.inner
        self.rank = lax.axis_index(name)

    def send(self, x, d_outer, d_inner):
        n, m = self.outer, self.inner
        if d_outer % n == 0 and d_inner % m == 0:
            return x
        pairs = [
            (i, ((i // m + d_outer) % n) * m + (i % m + d_inner) % m) for i in range(self.size)
        ]
        return lax.ppermute(x, self.name, pairs)

    def shifts(self):
        return [(a, b) for a in range(self.outer) for b in range(self.inner)]

    def source(self, a, b):
        n, m = self.outer, self.inner
        return ((self.rank // m + n - a) % n) * m + (self.rank % m + m - b) % m

    def gather(self, x):
        out = []
        for a in range(self.outer):
            far = self.send(x, a, 0)
            for b in range(self.inner):
                out.append(self.send(far, 0, b))
        return out

    def scatter(self, blocks):
        n, m = self.outer, self.inner
        near = {}
        for a in range(n):
            total = blocks[a * m].astype(f32)
            for b in range(1, m):
                total = total + self.send(blocks[a * m + b].astype(bf), 0, m - b).astype(f32)
            near[a] = total
        total = near[0]
        for a in range(1, n):
            total = total + self.send(near[a].astype(bf), n - a, 0).astype(f32)
        return total


def unpack_kernel(count, rows, parts, where_ref, *refs):
    mine, other, outs = refs[:count], refs[count : 2 * count], refs[2 * count :]
    piece = mine[0].shape[0]

    def put(low, high):
        for i in range(count):
            block = where_ref[i]
            start = 0
            for size, out in zip(parts, outs):
                for at, ref in ((0, low[i]), (piece, high[i])):
                    lo, hi = max(start, at), min(start + size, at + piece)
                    if lo < hi:
                        to = pl.multiple_of(block * size + (lo - start), 8)
                        out[pl.ds(to, hi - lo), :] = ref[lo - at : hi - at, :]
                start += size

    @pl.when(where_ref[count] == 0)
    def _():
        put(mine, other)

    @pl.when(where_ref[count] != 0)
    def _():
        put(other, mine)


def unpack(mine, other, where, parts):
    count = len(mine)
    width = mine[0].shape[1]
    return pl.pallas_call(
        functools.partial(unpack_kernel, count, sum(parts), parts),
        out_shape=[jax.ShapeDtypeStruct((count * size, width), bf) for size in parts],
        in_specs=[pl.BlockSpec(memory_space=pltpu.SMEM)]
        + [pl.BlockSpec(memory_space=pltpu.VMEM)] * (2 * count),
        out_specs=[pl.BlockSpec(memory_space=pltpu.VMEM)] * len(parts),
    )(where, *mine, *other)


def after(x, *deps):
    return lax.optimization_barrier((x,) + deps)[0]


def shards(
    layer_input,
    out_cotangent,
    block_pairs,
    w_query,
    w_key,
    w_value,
    w_output,
    w_gate,
    w_up,
    w_down,
    input_gain,
    attnpost_gain,
    ffnpre_gain,
    ffnpost_gain,
    query_gain,
    key_gain,
):
    S, C = Axis("shard"), Axis("ctx")
    seqs_here, rows_two, width = layer_input.shape
    blk = rows_two // 2
    row_count = seqs_here * rows_two
    rank = C.rank
    twin = C.rank % C.inner
    head_size = query_gain.shape[0] * S.size
    heads = w_query.shape[1] * S.size // head_size
    pq, pk, po = w_query.shape[1], w_key.shape[1], w_output.shape[0]
    pf = w_down.shape[0]
    scale = head_size ** (-0.5)

    small = [input_gain, attnpost_gain, ffnpre_gain, ffnpost_gain, query_gain, key_gain]
    rows = [
        lax.dynamic_update_slice(jnp.zeros((width,), bf), g, (S.rank * g.shape[0],)) for g in small
    ]
    gain_rows = jnp.concatenate([jnp.stack(rows), jnp.zeros((16 - len(rows), width), bf)], axis=0)

    qkv = jnp.concatenate([w_query.T, w_key.T, w_value.T], axis=0)

    def half_of(x, which):
        piece = x.shape[0] // C.inner
        return lax.dynamic_slice_in_dim(x, which * piece, piece, 0)

    where = jnp.stack([S.source(a, b) for a, b in S.shifts()] + [twin]).astype(jnp.int32)
    first = jnp.concatenate([half_of(qkv, twin), gain_rows], axis=0)
    got_qkv = S.gather(first)
    near_qkv = [C.send(x, 0, 1) for x in got_qkv]
    gains = sum([x[-16:].astype(f32) for x in got_qkv])
    g_in, g_pa, g_pf, g_po = [gains[i] for i in range(4)]
    g_q, g_k = gains[4, :head_size], gains[5, :head_size]
    piece = qkv.shape[0] // C.inner
    wq_t, wk_t, wv_t = unpack(
        [x[:piece] for x in got_qkv], [x[:piece] for x in near_qkv], where, (pq, pk, pk)
    )

    got_o = S.gather(after(half_of(w_output, twin), got_qkv[-1]))
    near_o = [C.send(x, 0, 1) for x in got_o]
    (wo_all,) = unpack(got_o, near_o, where, (po,))

    pc = pf // C.size

    def part_of(x):
        return lax.dynamic_slice_in_dim(x, rank * pc, pc, 0)

    ffn = jnp.concatenate([part_of(w_gate.T), part_of(w_up.T), part_of(w_down)], axis=0)
    got_f = S.gather(after(ffn, got_o[-1]))
    wg_t = jnp.concatenate([x[:pc] for x in got_f], axis=0)
    wu_t = jnp.concatenate([x[pc : 2 * pc] for x in got_f], axis=0)
    wd = jnp.concatenate([x[2 * pc :] for x in got_f], axis=0)

    def times(a, b):
        return lax.dot_general(a, b, (((1,), (0,)), ((), ())), preferred_element_type=f32)

    def times_t(a, b):
        return lax.dot_general(a, b, (((1,), (1,)), ((), ())), preferred_element_type=f32)

    def t_times(a, b):
        return lax.dot_general(a, b, (((0,), (0,)), ((), ())), preferred_element_type=f32)

    key_pos = seq_positions(block_pairs, blk)
    query_pos = lax.dynamic_slice_in_dim(key_pos, rank * rows_two, rows_two, axis=1)
    cosine, sine = rope_tables(query_pos, head_size)
    q_cos = cosine[:, :, None, :]
    q_sin = sine[:, :, None, :]
    order = [C.source(a, b) for a, b in C.shifts()]
    key_pos = jnp.concatenate(
        [lax.dynamic_slice_in_dim(key_pos, o * rows_two, rows_two, axis=1) for o in order], axis=1
    )
    mask = key_pos[:, None, None, :] <= query_pos[:, None, :, None]
    x_f = layer_input.reshape(row_count, width).astype(f32)
    normed_in = norm_rows(x_f, g_in).astype(bf)
    query_raw = times_t(normed_in, wq_t).reshape(seqs_here, rows_two, heads, head_size)
    key_raw = times_t(normed_in, wk_t).reshape(seqs_here, rows_two, head_size)
    values_loc = times_t(normed_in, wv_t).astype(bf).reshape(seqs_here, rows_two, head_size)
    query_rot = head_prep(query_raw, g_q, q_cos, q_sin).astype(bf)
    key_rot = head_prep(key_raw, g_k, cosine, sine).astype(bf)
    kv = C.gather(jnp.concatenate([key_rot, values_loc], axis=-1))
    kv = jnp.concatenate(kv, axis=1)
    keys_all, values_all = kv[..., :head_size], kv[..., head_size:]

    scores = jnp.einsum("sqhd,skd->shqk", query_rot, keys_all, preferred_element_type=f32) * scale
    scores = jnp.where(mask, scores, -1e30)
    top = jnp.max(scores, axis=-1, keepdims=True)
    lse = top + jnp.log(jnp.sum(jnp.exp(scores - top), axis=-1, keepdims=True))
    probs32 = jnp.exp(scores - lse)
    probs = probs32.astype(bf)
    attended = jnp.einsum("shqk,skd->sqhd", probs, values_all, preferred_element_type=f32)
    attended = attended.reshape(row_count, heads * head_size).astype(bf)
    projected = times(attended, wo_all)
    resid = x_f + norm_rows(projected, g_pa)
    normed_loc = norm_rows(resid, g_pf).astype(bf)

    normed_mid = jnp.concatenate(C.gather(normed_loc), axis=0)
    gate = times_t(normed_mid, wg_t)
    upward = times_t(normed_mid, wu_t)
    hidden = gated_unit(gate, upward).astype(bf)

    def back_home(partial):
        blocks = partial.reshape((C.size, row_count) + partial.shape[1:])
        return C.scatter([blocks[i] for i in range(C.size)])

    ffn_out = back_home(times(hidden, wd))
    layer_output = (resid + norm_rows(ffn_out, g_po)).astype(bf).reshape(seqs_here, rows_two, width)
    cot = out_cotangent.reshape(row_count, width).astype(f32)
    unused, pull = jax.vjp(norm_rows, ffn_out, g_po)
    d_ffn, dg_po = pull(cot)
    d_ffn_b = jnp.concatenate(C.gather(d_ffn.astype(bf)), axis=0)
    d_hidden = times_t(d_ffn_b, wd)
    unused, pull = jax.vjp(gated_unit, gate, upward)
    d_gate, d_upward = pull(d_hidden)
    d_gate = d_gate.astype(bf)
    d_upward = d_upward.astype(bf)
    d_mid = back_home(times(d_gate, wg_t) + times(d_upward, wu_t))
    gw_f = [
        g.astype(bf).reshape(S.size, pc, width)
        for g in (
            t_times(d_gate, normed_mid),
            t_times(d_upward, normed_mid),
            t_times(hidden, d_ffn_b),
        )
    ]
    gw_f = jnp.concatenate(gw_f, axis=1)
    part_f = S.scatter([gw_f[i] for i in range(S.size)]).astype(bf)
    all_f = lax.all_gather(part_f, "ctx", axis=0, tiled=False).astype(f32)
    out_gate = all_f[:, :pc].reshape(pf, width).T
    out_up = all_f[:, pc : 2 * pc].reshape(pf, width).T
    out_down = all_f[:, 2 * pc :].reshape(pf, width)

    unused, pull = jax.vjp(norm_rows, resid, g_pf)
    d_resid_n, dg_pf = pull(d_mid)
    d_resid = cot + d_resid_n
    unused, pull = jax.vjp(norm_rows, projected, g_pa)
    d_projected, dg_pa = pull(d_resid)
    d_proj_b = d_projected.astype(bf)

    def total_of(grad, rows_each):
        grad = grad.reshape(S.size, rows_each, width)
        piece = rows_each // C.inner
        blocks = []
        for a, b in S.shifts():
            block = lax.dynamic_index_in_dim(grad, S.source(a, b), 0, keepdims=False)
            keep = half_of(block, twin).astype(f32)
            for d in range(1, C.inner):
                give = half_of(block, (twin + d) % C.inner)
                keep = keep + C.send(give.astype(bf), 0, d).astype(f32)
            blocks.append(keep)
        mine = S.scatter(blocks)
        out = mine
        for a in range(1, C.outer):
            out = out + C.send(mine.astype(bf), a, 0).astype(f32)
        if C.inner == 1:
            return out
        out = out.astype(bf)
        other = C.send(out, 0, 1)
        low = jnp.where(twin == 0, out, other)
        high = jnp.where(twin == 0, other, out)
        return jnp.concatenate([low, high], axis=0).astype(f32)

    out_output = total_of(t_times(attended, d_proj_b).astype(bf), po)

    d_attended = times_t(d_proj_b, wo_all).astype(bf)
    d_attended = d_attended.reshape(seqs_here, rows_two, heads, head_size)
    d_probs = jnp.einsum("sqhd,skd->shqk", d_attended, values_all, preferred_element_type=f32)
    delta = jnp.sum(probs32 * d_probs, axis=-1, keepdims=True)
    d_scores = (probs32 * (d_probs - delta) * scale).astype(bf)
    d_query_rot = jnp.einsum("shqk,skd->sqhd", d_scores, keys_all, preferred_element_type=f32)
    key_part = jnp.einsum("shqk,sqhd->skd", d_scores, query_rot, preferred_element_type=f32)
    value_part = jnp.einsum("shqk,sqhd->skd", probs, d_attended, preferred_element_type=f32)
    kv_part = jnp.concatenate([key_part, value_part], axis=-1).astype(bf)
    kv_part = kv_part.reshape(seqs_here, C.size, rows_two, 2 * head_size)
    d_kv = C.scatter([kv_part[:, i] for i in range(C.size)])
    d_key_rot, d_values = d_kv[..., :head_size], d_kv[..., head_size:]
    d_values = d_values.astype(bf).reshape(row_count, head_size)
    unused, pull = jax.vjp(
        lambda raw, scaling: head_prep(raw, scaling, q_cos, q_sin), query_raw, g_q
    )
    d_query, dg_q = pull(d_query_rot)
    d_query = d_query.astype(bf).reshape(row_count, heads * head_size)
    out_query = total_of(t_times(d_query, normed_in).astype(bf), pq).T
    unused, pull = jax.vjp(lambda raw, scaling: head_prep(raw, scaling, cosine, sine), key_raw, g_k)
    d_key, dg_k = pull(d_key_rot)
    d_key = d_key.astype(bf).reshape(row_count, head_size)
    d_in = times(d_query, wq_t) + times(d_key, wk_t) + times(d_values, wv_t)
    unused, pull = jax.vjp(norm_rows, x_f, g_in)
    d_x_n, dg_in = pull(d_in)
    input_grad = (d_resid + d_x_n).reshape(seqs_here, rows_two, width)

    pieces = [g.reshape(S.size, -1) for g in (dg_in, dg_pa, dg_pf, dg_po, dg_q, dg_k)]
    flat = jnp.concatenate(pieces, axis=1)
    flat = jnp.pad(flat, ((0, 0), (0, -flat.shape[1] % width)))
    flat = flat.reshape(S.size, -1, width)
    flat = jnp.pad(flat, ((0, 0), (0, -flat.shape[1] % 16), (0, 0)))
    last = jnp.concatenate(
        [
            t_times(d_key, normed_in).reshape(S.size, pk, width),
            t_times(d_values, normed_in).reshape(S.size, pk, width),
            flat,
        ],
        axis=1,
    ).astype(bf)
    last = total_of(last, last.shape[1])
    out_key = last[:pk].T
    out_value = last[pk : 2 * pk].T
    tail = last[2 * pk :].reshape(-1)
    sums = []
    at = 0
    for g in small:
        sums.append(tail[at : at + g.shape[0]])
        at += g.shape[0]
    return (
        layer_output,
        input_grad,
        out_query,
        out_key,
        out_value,
        out_output,
        out_gate,
        out_up,
        out_down,
        *sums,
    )


def solution(mesh):
    rows = P("shard", "ctx", None)
    cols = P(None, "shard")
    lead = P("shard", None)
    gain = P("shard")
    return jax.shard_map(
        shards,
        mesh=mesh,
        in_specs=(rows, rows, lead, cols, cols, cols, lead, cols, cols, lead) + (gain,) * 6,
        out_specs=(rows, rows, cols, cols, cols, lead, cols, cols, lead) + (gain,) * 6,
        check_vma=False,
    )
```

```python
import functools

import jax
import jax.numpy as jnp
from jax import lax
from jax.experimental import pallas as pl
from jax.experimental.pallas import tpu as pltpu
from jax.sharding import PartitionSpec as P


epsilon = 1e-06
rope_base = 1000000.0
bf = jnp.bfloat16
f32 = jnp.float32
root = 0.7978845608028654
cubic = 0.044715


class Axis:
    def __init__(self, name):
        self.name = name
        self.size = lax.axis_size(name)
        assert self.size % 2 == 0
        self.inner = 2
        self.outer = self.size // 2
        self.rank = lax.axis_index(name)

    def send(self, x, d_outer, d_inner):
        n, m = self.outer, self.inner
        pairs = [
            (i, ((i // m + d_outer) % n) * m + (i % m + d_inner) % m) for i in range(self.size)
        ]
        return lax.ppermute(x, self.name, pairs)

    def shifts(self):
        return [(a, b) for a in range(self.outer) for b in range(self.inner)]

    def sources(self):
        n, m = self.outer, self.inner
        return [
            ((self.rank // m + n - a) % n) * m + (self.rank % m + m - b) % m
            for a, b in self.shifts()
        ]

    def gather(self, x):
        out = []
        for a in range(self.outer):
            far = self.send(x, a, 0) if a else x
            out += [far, self.send(far, 0, 1)]
        return out


def times(a, b):
    return lax.dot_general(a, b, (((1,), (0,)), ((), ())), preferred_element_type=f32)


def times_t(a, b):
    return lax.dot_general(a, b, (((1,), (1,)), ((), ())), preferred_element_type=f32)


def t_times(a, b):
    return lax.dot_general(a, b, (((0,), (0,)), ((), ())), preferred_element_type=f32)


def inverse_rms(v):
    return lax.rsqrt(jnp.mean(v * v, axis=-1, keepdims=True) + epsilon)


def norm(v, g):
    return v * inverse_rms(v) * g


def norm_back(v, g, dy):
    r = inverse_rms(v)
    gd = g * dy
    dv = r * gd - v * (r * r * r) * jnp.mean(v * gd, axis=-1, keepdims=True)
    return dv, jnp.sum(dy * v * r, axis=0, keepdims=True)


def call(body, outs, args, scalars=0, scratch=()):
    vmem = pl.BlockSpec(memory_space=pltpu.VMEM)
    smem = pl.BlockSpec(memory_space=pltpu.SMEM)
    return pl.pallas_call(
        body,
        out_shape=[jax.ShapeDtypeStruct(shape, kind) for shape, kind in outs],
        in_specs=[smem] * scalars + [vmem] * (len(args) - scalars),
        out_specs=[vmem] * len(outs),
        scratch_shapes=list(scratch),
    )(*args)


def rope_tables(positions, width):
    half = width // 2
    index = jnp.arange(half).astype(f32)
    freq = jnp.power(rope_base, -(2.0 * index) / width)
    angle = positions.astype(f32)[..., None] * freq
    return (jnp.cos(angle), jnp.sin(angle))


def seq_positions(pairs, blk):
    count = pairs.shape[-1]
    offset = jnp.arange(2 * blk, dtype=jnp.int32)
    chosen = pairs[..., None]
    block = jnp.where(offset < blk, chosen, 2 * count - 1 - chosen)
    return block * blk + offset % blk


def after(x, *deps):
    return lax.optimization_barrier((x,) + deps)[0]


def unpack(where, mine, other, piece, outs):
    count = len(mine)

    def put(low, high):
        for i in range(count):
            block = where[i]
            start = 0
            for out in outs:
                size = out.shape[0] // count
                for at, ref in ((0, low[i]), (piece, high[i])):
                    lo, hi = max(start, at), min(start + size, at + piece)
                    if lo < hi:
                        to = pl.multiple_of(block * size + (lo - start), 16)
                        out[pl.ds(to, hi - lo), :] = ref[lo - at : hi - at, :]
                start += size

    @pl.when(where[count] == 0)
    def _():
        put(mine, other)

    @pl.when(where[count] != 0)
    def _():
        put(other, mine)


def qkv_kernel(count, heads, where, x, cosine, sine, *refs):
    mine, other = refs[:count], refs[count : 2 * count]
    wq, wk, wv, gains, nin, qraw, kraw, qrot, kv = refs[2 * count :]
    piece = (wq.shape[0] + wk.shape[0] + wv.shape[0]) // count // 2
    hd = wk.shape[0]
    unpack(where, mine, other, piece, (wq, wk, wv))
    total = mine[0][piece:, :].astype(f32)
    for i in range(1, count):
        total = total + mine[i][piece:, :].astype(f32)
    gains[...] = total[: gains.shape[0], :]
    normed = norm(x[...].astype(f32), gains[0:1, :]).astype(bf)
    nin[...] = normed
    c, s = cosine[...], sine[...]
    half = hd // 2

    def turn(u):
        a, b = u[:, :half], u[:, half:]
        return a * c - b * s, b * c + a * s

    for h in range(heads):
        raw = times_t(normed, wq[h * hd : (h + 1) * hd, :])
        qraw[:, h * hd : (h + 1) * hd] = raw
        a, b = turn(norm(raw, gains[4:5, :hd]))
        qrot[:, h * hd : h * hd + half] = a.astype(bf)
        qrot[:, h * hd + half : (h + 1) * hd] = b.astype(bf)
    raw = times_t(normed, wk[...])
    kraw[...] = raw
    a, b = turn(norm(raw, gains[5:6, :hd]))
    kv[:, :half] = a.astype(bf)
    kv[:, half:hd] = b.astype(bf)
    kv[:, hd:] = times_t(normed, wv[...]).astype(bf)


def stacked(ref, rows, heads, hd):
    return jnp.concatenate([ref[rows, h * hd : (h + 1) * hd] for h in range(heads)], axis=0)


def attend_kernel(seqs, heads, scale, count, where, qpos, kpos, qrot, x, gains, *refs):
    mine, other, blocks = refs[:count], refs[count : 2 * count], refs[2 * count : -7]
    att, probs, kall, proj, resid, nmid, wo = refs[-7:]
    unpack(where, mine, other, mine[0].shape[0], (wo,))
    hd = kall.shape[1] // 2
    span = qrot.shape[0] // seqs
    length = len(blocks) * span
    for s in range(seqs):
        rows = slice(s * span, (s + 1) * span)
        for i, block in enumerate(blocks):
            kall[s * length + i * span : s * length + (i + 1) * span, :] = block[rows, :]
        keys = kall[s * length : (s + 1) * length, :hd]
        values = kall[s * length : (s + 1) * length, hd:]
        scores = times_t(stacked(qrot, rows, heads, hd), keys) * scale
        at = jnp.concatenate([qpos[rows, :]] * heads, axis=0)
        scores = jnp.where(kpos[s : s + 1, :] <= at, scores, -1e30)
        top = jnp.max(scores, axis=-1, keepdims=True)
        raised = jnp.exp(scores - top)
        p = raised / jnp.sum(raised, axis=-1, keepdims=True)
        probs[s * heads * span : (s + 1) * heads * span, :] = p
        out = times(p.astype(bf), values).astype(bf)
        for h in range(heads):
            att[rows, h * hd : (h + 1) * hd] = out[h * span : (h + 1) * span, :]
    projected = times(att[...], wo[...])
    proj[...] = projected
    r = x[...].astype(f32) + norm(projected, gains[1:2, :])
    resid[...] = r
    nmid[...] = norm(r, gains[2:3, :]).astype(bf)


def split(partial, count, keep, give):
    rows = partial.shape[0] // count
    for i in range(count):
        to = slice((i // 2) * rows, (i // 2 + 1) * rows)
        ref = give if i % 2 else keep
        ref[to, :] = partial[i * rows : (i + 1) * rows, :].astype(ref.dtype)


def ffn_kernel(count, members, *refs):
    chunks, blocks = refs[:count], refs[count : count + members]
    wg, wu, wd, nm, gate, up, hidden, keep, give = refs[count + members :]
    pc = wg.shape[0] // count
    rows = blocks[0].shape[0]
    for i in range(count):
        wg[i * pc : (i + 1) * pc, :] = chunks[i][:pc, :]
        wu[i * pc : (i + 1) * pc, :] = chunks[i][pc : 2 * pc, :]
        wd[i * pc : (i + 1) * pc, :] = chunks[i][2 * pc :, :]
    for i in range(members):
        nm[i * rows : (i + 1) * rows, :] = blocks[i][...]
    g = times_t(nm[...], wg[...])
    u = times_t(nm[...], wu[...])
    gate[...] = g
    up[...] = u
    t = jnp.tanh(root * (g + cubic * (g * g * g)))
    hid = (0.5 * g * (1.0 + t) * u).astype(bf)
    hidden[...] = hid
    split(times(hid, wd[...]), members, keep, give)


def ffn_end_kernel(keep, gave, resid, cot, gains, *refs):
    far, (out, d_ffn, dg) = refs[:-3], refs[-3:]
    rows = resid.shape[0]
    total = keep[:rows, :] + gave[:rows, :].astype(f32)
    for ref in far:
        total = total + ref[...].astype(f32)
    g = gains[3:4, :]
    out[...] = (resid[...] + norm(total, g)).astype(bf)
    d, dg[...] = norm_back(total, g, cot[...].astype(f32))
    d_ffn[...] = d.astype(bf)


def ffn_back_kernel(members, wg, wu, wd, gate, up, *refs):
    blocks = refs[:members]
    dall, dgate, dup, keep, give = refs[members:]
    rows = blocks[0].shape[0]
    for i in range(members):
        dall[i * rows : (i + 1) * rows, :] = blocks[i][...]
    d_hidden = times_t(dall[...], wd[...])
    g, u = gate[...], up[...]
    t = jnp.tanh(root * (g + cubic * (g * g * g)))
    slope = 0.5 * (1.0 + t) + 0.5 * g * (1.0 - t * t) * (root * (1.0 + 3.0 * cubic * (g * g)))
    dg = (d_hidden * u * slope).astype(bf)
    du = (d_hidden * (0.5 * g * (1.0 + t))).astype(bf)
    dgate[...] = dg
    dup[...] = du
    split(times(dg, wg[...]) + times(du, wu[...]), members, keep, give)


def ffn_grad_kernel(count, nm, dall, dgate, dup, hidden, keep, give):
    pc = hidden.shape[1] // count
    for k, (a, b) in enumerate(((dgate, nm), (dup, nm), (hidden, dall))):
        grad = t_times(a[...], b[...])
        for i in range(count):
            at = (i // 2) * 3 * pc + k * pc
            ref = give if i % 2 else keep
            ref[at : at + pc, :] = grad[i * pc : (i + 1) * pc, :].astype(ref.dtype)


def attend_back_kernel(seqs, heads, scale, keep, gave, resid, proj, cot, gains, wo, *refs):
    far = refs[:-11]
    probs, kall, qrot, d_resid, d_proj, dqrot, kkeep, kgive, dg_pf, dg_pa, dkall = refs[-11:]
    rows = resid.shape[0]
    hd = kall.shape[1] // 2
    span = rows // seqs
    length = kall.shape[0] // seqs
    total = keep[:rows, :] + gave[:rows, :].astype(f32)
    for ref in far:
        total = total + ref[...].astype(f32)
    d, dg_pf[...] = norm_back(resid[...], gains[2:3, :], total)
    d = d + cot[...].astype(f32)
    d_resid[...] = d
    d, dg_pa[...] = norm_back(proj[...], gains[1:2, :], d)
    d = d.astype(bf)
    d_proj[...] = d
    d_att = times_t(d, wo[...]).astype(bf)
    for s in range(seqs):
        at = slice(s * span, (s + 1) * span)
        keys = kall[s * length : (s + 1) * length, :hd]
        values = kall[s * length : (s + 1) * length, hd:]
        p = probs[s * heads * span : (s + 1) * heads * span, :]
        da = jnp.concatenate([d_att[at, h * hd : (h + 1) * hd] for h in range(heads)], axis=0)
        dp = times_t(da, values)
        delta = jnp.sum(p * dp, axis=-1, keepdims=True)
        ds = (p * (dp - delta) * scale).astype(bf)
        dq = times(ds, keys)
        for h in range(heads):
            dqrot[at, h * hd : (h + 1) * hd] = dq[h * span : (h + 1) * span, :]
        dkall[:, :hd] = t_times(ds, stacked(qrot, at, heads, hd))
        dkall[:, hd:] = t_times(p.astype(bf), da)
        for i in range(length // span):
            ref = kgive if i % 2 else kkeep
            to = (i // 2) * rows + s * span
            ref[to : to + span, :] = dkall[i * span : (i + 1) * span, :].astype(ref.dtype)


def unturn(d, c, s):
    half = d.shape[1] // 2
    a, b = d[:, :half], d[:, half:]
    return jnp.concatenate([a * c + b * s, b * c - a * s], axis=1)


def packed(count, where, sources, keep, give, tail=None):
    twin = where[count]
    sizes = [src.shape[0] // count // 2 for src in sources]
    each = sum(sizes)
    for i in range(count):
        block = where[i]
        to = ((i % 2) * (count // 2) + i // 2) * each
        for src, size in zip(sources, sizes):
            own = pl.multiple_of(block * (2 * size) + twin * size, 8)
            their = pl.multiple_of(block * (2 * size) + (1 - twin) * size, 8)
            keep[to : to + size, :] = src[pl.ds(own, size), :].astype(keep.dtype)
            give[to : to + size, :] = src[pl.ds(their, size), :].astype(bf)
            to += size
    if tail is not None:
        keep[count * each :, :] = tail.astype(keep.dtype)
        give[count * each :, :] = tail.astype(bf)


def query_back_kernel(
    count, heads, where, dqrot, qraw, gains, cosine, sine, nin, att, d_proj, dq, dg_q, keep, give, gq, go
):
    hd = qraw.shape[1] // heads
    c, s = cosine[...], sine[...]
    total = jnp.zeros((1, hd), f32)
    for h in range(heads):
        at = slice(h * hd, (h + 1) * hd)
        d, dg = norm_back(qraw[:, at], gains[4:5, :hd], unturn(dqrot[:, at], c, s))
        dq[:, at] = d.astype(bf)
        total = total + dg
    dg_q[...] = total
    gq[...] = t_times(dq[...], nin[...])
    go[...] = t_times(att[...], d_proj[...])
    packed(count, where, (gq, go), keep, give)


def key_back_kernel(
    count, where, kkeep, kgave, kraw, gains, cosine, sine, nin, dq, wq, wk, wv, x, d_resid, dg_po, dg_pf, dg_pa, dg_q, *refs
):
    far, (grad, keep, give, gk, gv) = refs[:-5], refs[-5:]
    rows, hd = kraw.shape
    total = kkeep[:rows, :] + kgave[:rows, :].astype(f32)
    for ref in far:
        total = total + ref[...].astype(f32)
    d, dg_k = norm_back(
        kraw[...], gains[5:6, :hd], unturn(total[:, :hd], cosine[...], sine[...])
    )
    dk = d.astype(bf)
    dv = total[:, hd:].astype(bf)
    d_in = times(dq[...], wq[...]) + times(dk, wk[...]) + times(dv, wv[...])
    d, dg_in = norm_back(x[...].astype(f32), gains[0:1, :], d_in)
    grad[...] = d_resid[...] + d
    gk[...] = t_times(dk, nin[...])
    gv[...] = t_times(dv, nin[...])
    pad = jnp.zeros((1, nin.shape[1] - hd), f32)
    none = jnp.zeros((2, nin.shape[1]), f32)
    tail = jnp.concatenate(
        [
            dg_in,
            dg_pa[...],
            dg_pf[...],
            dg_po[...],
            jnp.concatenate([dg_q[...], pad], axis=1),
            jnp.concatenate([dg_k, pad], axis=1),
            none,
        ],
        axis=0,
    )
    packed(count, where, (gk, gv), keep, give, tail)


def near_kernel(half, keep, gave, keep2, give2):
    tail = keep.shape[0] - 2 * half
    keep2[:half, :] = keep[:half, :].astype(f32) + gave[:half, :].astype(f32)
    rest = slice(half, 2 * half)
    give2[:half, :] = (keep[rest, :].astype(f32) + gave[rest, :].astype(f32)).astype(bf)
    if tail:
        t = keep[2 * half :, :].astype(f32) + gave[2 * half :, :].astype(f32)
        keep2[half:, :] = t
        give2[half:, :] = t.astype(bf)


def far_kernel(parts, rows, keep, gave, *outs):
    tail = keep.shape[0] - parts * rows
    for a in range(parts):
        at = slice(a * rows, (a + 1) * rows)
        outs[a][:rows, :] = (keep[at, :].astype(f32) + gave[at, :].astype(f32)).astype(outs[a].dtype)
    if tail:
        at = slice(parts * rows, parts * rows + tail)
        t = keep[at, :].astype(f32) + gave[at, :].astype(f32)
        for a in range(parts):
            outs[a][rows:, :] = t.astype(outs[a].dtype)


def ffn_out_kernel(members, where, *refs):
    blocks, (gate, up, down, buf) = refs[:members], refs[members:]
    pc = blocks[0].shape[0] // 3
    for k, out in enumerate((gate, up, down)):
        to_ref = out if k == 2 else buf
        for i in range(members):
            to = pl.multiple_of(where[i] * pc, 8)
            to_ref[pl.ds(to, pc), :] = blocks[i][k * pc : (k + 1) * pc, :].astype(f32)
        if k < 2:
            out[...] = buf[...].T


def joined(sizes, twin, mine, other, outs):
    def put(low, high):
        start = 0
        for size, out in zip(sizes, outs):
            half = size // 2
            rows = slice(start, start + half)
            start += half
            if out.shape[0] != size:
                out[...] = jnp.concatenate([low[rows, :], high[rows, :]], axis=0).astype(f32).T
            else:
                out[:half, :] = low[rows, :].astype(f32)
                out[half:, :] = high[rows, :].astype(f32)

    @pl.when(twin == 0)
    def _():
        put(mine, other)

    @pl.when(twin != 0)
    def _():
        put(other, mine)


def query_out_kernel(sizes, twin, mine, other, *outs):
    joined(sizes, twin[0], mine, other, outs)


def key_out_kernel(sizes, at, mine, other, out_k, out_v, *gains):
    joined(sizes, at[0], mine, other, (out_k, out_v))
    tail = mine[mine.shape[0] - 8 :, :]
    for first, last in ((0, 4), (4, 6)):
        size = gains[first].shape[0]
        shape = (tail.shape[1], size)
        row = lax.broadcasted_iota(jnp.int32, shape, 0)
        col = lax.broadcasted_iota(jnp.int32, shape, 1)
        own = times(tail, (row == at[1] * size + col).astype(f32).astype(bf))
        for i in range(first, last):
            gains[i][...] = own[i, :]


def shards(
    layer_input,
    out_cotangent,
    block_pairs,
    w_query,
    w_key,
    w_value,
    w_output,
    w_gate,
    w_up,
    w_down,
    input_gain,
    attnpost_gain,
    ffnpre_gain,
    ffnpost_gain,
    query_gain,
    key_gain,
):
    S, C = Axis("shard"), Axis("ctx")
    seqs, span, width = layer_input.shape
    rows = seqs * span
    members, count = C.size, S.size
    twin = C.rank % 2
    pq, pk, po, pf = w_query.shape[1], w_key.shape[1], w_output.shape[0], w_down.shape[0]
    hd = query_gain.shape[0] * count
    hq = pq * count
    heads = hq // hd
    scale = hd ** (-0.5)
    where = jnp.stack(S.sources() + [twin]).astype(jnp.int32)
    x = layer_input.reshape(rows, width)
    cot = out_cotangent.reshape(rows, width)

    small = [input_gain, attnpost_gain, ffnpre_gain, ffnpost_gain, query_gain, key_gain]

    def placed(same):
        size = same[0].shape[0]
        at = jnp.arange(width)[None, :] == S.rank * size + jnp.arange(size)[:, None]
        return times(jnp.stack(same), at.astype(bf)).astype(bf)

    gain_rows = jnp.concatenate([placed(small[:4]), placed(small[4:])], axis=0)
    gain_rows = jnp.pad(gain_rows, ((0, 8 - len(small)), (0, 0)))

    whole = jnp.concatenate([w_query.T, w_key.T, w_value.T], axis=0)
    piece = whole.shape[0] // 2
    own = jnp.where(twin == 0, whole[:piece], whole[piece:])
    first = jnp.concatenate([own, gain_rows], axis=0)
    mine = S.gather(first)
    other = [C.send(m, 0, 1) for m in mine]
    own = lax.dynamic_slice_in_dim(w_output, twin * (po // 2), po // 2, 0)
    mine_o = S.gather(after(own, *mine[2::2]))
    other_o = [C.send(m, 0, 1) for m in mine_o]

    pc = pf // members

    def part_of(w):
        return lax.dynamic_slice_in_dim(w, C.rank * pc, pc, 0)

    ffn = jnp.concatenate([part_of(w_gate.T), part_of(w_up.T), part_of(w_down)], axis=0)
    chunks = S.gather(after(ffn, *mine_o[2::2]))

    places = seq_positions(block_pairs, span // 2)
    kpos = jnp.concatenate(
        [lax.dynamic_index_in_dim(places, o, 1, keepdims=False) for o in C.sources()], axis=1
    )
    own_pos = lax.dynamic_index_in_dim(places, C.rank, 1, keepdims=False).reshape(rows)
    cosine, sine = rope_tables(own_pos, hd)
    qpos = own_pos[:, None]

    wq, wk, wv, gains, nin, qraw, kraw, qrot, kv = call(
        functools.partial(qkv_kernel, count, heads),
        [
            ((hq, width), bf),
            ((hd, width), bf),
            ((hd, width), bf),
            ((8, width), f32),
            ((rows, width), bf),
            ((rows, hq), f32),
            ((rows, hd), f32),
            ((rows, hq), bf),
            ((rows, 2 * hd), bf),
        ],
        (where, x, cosine, sine, *mine, *other),
        scalars=1,
    )
    kvs = C.gather(kv)
    length = members * span
    att, probs, kall, proj, resid, nmid, wo = call(
        functools.partial(attend_kernel, seqs, heads, scale, count),
        [
            ((rows, hq), bf),
            ((seqs * heads * span, length), f32),
            ((seqs * length, 2 * hd), bf),
            ((rows, width), f32),
            ((rows, width), f32),
            ((rows, width), bf),
            ((hq, width), bf),
        ],
        (where, qpos, kpos, qrot, x, gains, *mine_o, *other_o, *kvs),
        scalars=1,
    )
    hid = count * pc
    wg, wu, wd, nm, gate, up, hidden, keep, give = call(
        functools.partial(ffn_kernel, count, members),
        [
            ((hid, width), bf),
            ((hid, width), bf),
            ((hid, width), bf),
            ((members * rows, width), bf),
            ((members * rows, hid), f32),
            ((members * rows, hid), f32),
            ((members * rows, hid), bf),
            ((C.outer * rows, width), f32),
            ((C.outer * rows, width), bf),
        ],
        (*chunks, *C.gather(nmid)),
    )

    def home(keep, give):
        gave = C.send(give, 0, 1)
        far = []
        for a in range(1, C.outer):
            at = slice(a * rows, (a + 1) * rows)
            part = (keep[at] + gave[at].astype(f32)).astype(bf)
            far.append(C.send(part, C.outer - a, 0))
        return gave, far

    gave, far = home(keep, give)
    layer_output, d_ffn, dg_po = call(
        ffn_end_kernel,
        [((rows, width), bf), ((rows, width), bf), ((1, width), f32)],
        (keep, gave, resid, cot, gains, *far),
    )
    dall, dgate, dup, keep, give = call(
        functools.partial(ffn_back_kernel, members),
        [
            ((members * rows, width), bf),
            ((members * rows, hid), bf),
            ((members * rows, hid), bf),
            ((C.outer * rows, width), f32),
            ((C.outer * rows, width), bf),
        ],
        (wg, wu, wd, gate, up, *C.gather(d_ffn)),
    )
    gave, far = home(keep, give)

    def spread(keep, give, each):
        got = S.send(give, 0, 1)
        n = each + keep.shape[0] - S.outer * each
        parts = call(
            functools.partial(far_kernel, S.outer, each),
            [((n, width), f32)] + [((n, width), bf)] * (S.outer - 1),
            (keep, got),
        )
        return [parts[0]] + [S.send(parts[a], S.outer - a, 0) for a in range(1, S.outer)]

    def summed(terms):
        total = terms[0].astype(f32)
        for term in terms[1:]:
            total = total + term.astype(f32)
        return total.astype(bf)

    fkeep, fgive = call(
        functools.partial(ffn_grad_kernel, count),
        [((S.outer * 3 * pc, width), bf), ((S.outer * 3 * pc, width), bf)],
        (nm, dall, dgate, dup, hidden),
    )
    f_terms = spread(fkeep, fgive, 3 * pc)

    d_resid, d_proj, dqrot, kkeep, kgive, dg_pf, dg_pa = call(
        functools.partial(attend_back_kernel, seqs, heads, scale),
        [
            ((rows, width), f32),
            ((rows, width), bf),
            ((rows, hq), f32),
            ((C.outer * rows, 2 * hd), f32),
            ((C.outer * rows, 2 * hd), bf),
            ((1, width), f32),
            ((1, width), f32),
        ],
        (keep, gave, resid, proj, cot, gains, wo, *far, probs, kall, qrot),
        scratch=[pltpu.VMEM((length, 2 * hd), f32)],
    )
    kgave, kfar = home(kkeep, kgive)

    def begin(keep, give, each):
        got = C.send(give, 0, 1)
        half = S.outer * each
        n = keep.shape[0] - half
        keep, give = call(
            functools.partial(near_kernel, half), [((n, width), f32), ((n, width), bf)], (keep, got)
        )
        return spread(keep, give, each)

    def finish(terms):
        part = summed(terms)
        far = [C.send(part, a, 0) for a in range(1, C.outer)]
        total = summed([part] + far)
        return total, C.send(total, 0, 1)

    each_q, each_k = (pq + po) // 2, pk
    dq, dg_q, keep, give = call(
        functools.partial(query_back_kernel, count, heads),
        [
            ((rows, hq), bf),
            ((1, hd), f32),
            ((count * each_q, width), bf),
            ((count * each_q, width), bf),
        ],
        (where, dqrot, qraw, gains, cosine, sine, nin, att, d_proj),
        scalars=1,
        scratch=[pltpu.VMEM((hq, width), f32), pltpu.VMEM((hq, width), f32)],
    )
    q_terms = begin(keep, give, each_q)
    input_grad, keep, give = call(
        functools.partial(key_back_kernel, count),
        [
            ((rows, width), f32),
            ((count * each_k + 8, width), f32),
            ((count * each_k + 8, width), bf),
        ],
        (
            where,
            kkeep,
            kgave,
            kraw,
            gains,
            cosine,
            sine,
            nin,
            dq,
            wq,
            wk,
            wv,
            x,
            d_resid,
            dg_po,
            dg_pf,
            dg_pa,
            dg_q,
            *kfar,
        ),
        scalars=1,
        scratch=[pltpu.VMEM((hd, width), f32), pltpu.VMEM((hd, width), f32)],
    )
    k_terms = begin(keep, give, each_k)
    total_q = finish(q_terms)
    total_k = finish(k_terms)

    out_gate, out_up, out_down = call(
        functools.partial(ffn_out_kernel, members),
        [((width, pf), f32), ((width, pf), f32), ((pf, width), f32)],
        (jnp.stack(C.sources()).astype(jnp.int32), *C.gather(summed(f_terms))),
        scalars=1,
        scratch=[pltpu.VMEM((pf, width), f32)],
    )
    is_twin = twin.astype(jnp.int32)[None]
    out_query, out_output = call(
        functools.partial(query_out_kernel, (pq, po)),
        [((width, pq), f32), ((po, width), f32)],
        (is_twin, *total_q),
        scalars=1,
    )
    out_key, out_value, *sums = call(
        functools.partial(key_out_kernel, (pk, pk)),
        [((pk, width), f32), ((pk, width), f32)] + [(g.shape, f32) for g in small],
        (jnp.stack([twin, S.rank]).astype(jnp.int32), *total_k),
        scalars=1,
    )
    out_key, out_value = out_key.T, out_value.T
    return (
        layer_output.reshape(seqs, span, width),
        input_grad.reshape(seqs, span, width),
        out_query,
        out_key,
        out_value,
        out_output,
        out_gate,
        out_up,
        out_down,
        *sums,
    )


def solution(mesh):
    lead2 = P("shard", "ctx", None)
    cols = P(None, "shard")
    lead = P("shard", None)
    gain = P("shard")
    return jax.shard_map(
        shards,
        mesh=mesh,
        in_specs=(lead2, lead2, lead, cols, cols, cols, lead, cols, cols, lead) + (gain,) * 6,
        out_specs=(lead2, lead2, cols, cols, cols, lead, cols, cols, lead) + (gain,) * 6,
        check_vma=False,
    )
```

```python
import functools

import jax
import jax.numpy as jnp
from jax import lax
from jax.experimental import pallas as pl
from jax.experimental.pallas import tpu as pltpu
from jax.sharding import PartitionSpec as P


epsilon = 1e-06
rope_base = 1000000.0
bf = jnp.bfloat16
f32 = jnp.float32
root = 0.7978845608028654
cubic = 0.044715


class Axis:
    def __init__(self, name):
        self.name = name
        self.size = lax.axis_size(name)
        assert self.size % 2 == 0
        self.inner = 2
        self.outer = self.size // 2
        self.rank = lax.axis_index(name)

    def send(self, x, d_outer, d_inner):
        n, m = self.outer, self.inner
        pairs = [
            (i, ((i // m + d_outer) % n) * m + (i % m + d_inner) % m) for i in range(self.size)
        ]
        return lax.ppermute(x, self.name, pairs)

    def shifts(self):
        return [(a, b) for a in range(self.outer) for b in range(self.inner)]

    def sources(self):
        n, m = self.outer, self.inner
        return [
            ((self.rank // m + n - a) % n) * m + (self.rank % m + m - b) % m
            for a, b in self.shifts()
        ]

    def gather(self, x):
        out = []
        for a in range(self.outer):
            far = self.send(x, a, 0) if a else x
            out += [far, self.send(far, 0, 1)]
        return out


def times(a, b):
    return lax.dot_general(a, b, (((1,), (0,)), ((), ())), preferred_element_type=f32)


def times_t(a, b):
    return lax.dot_general(a, b, (((1,), (1,)), ((), ())), preferred_element_type=f32)


def t_times(a, b):
    return lax.dot_general(a, b, (((0,), (0,)), ((), ())), preferred_element_type=f32)


def inverse_rms(v):
    return lax.rsqrt(jnp.mean(v * v, axis=-1, keepdims=True) + epsilon)


def norm(v, g):
    return v * inverse_rms(v) * g


def norm_back(v, g, dy):
    r = inverse_rms(v)
    gd = g * dy
    dv = r * gd - v * (r * r * r) * jnp.mean(v * gd, axis=-1, keepdims=True)
    return dv, jnp.sum(dy * v * r, axis=0, keepdims=True)


def call(body, outs, args, scalars=0, scratch=()):
    vmem = pl.BlockSpec(memory_space=pltpu.VMEM)
    smem = pl.BlockSpec(memory_space=pltpu.SMEM)
    return pl.pallas_call(
        body,
        out_shape=[jax.ShapeDtypeStruct(shape, kind) for shape, kind in outs],
        in_specs=[smem] * scalars + [vmem] * (len(args) - scalars),
        out_specs=[vmem] * len(outs),
        scratch_shapes=list(scratch),
    )(*args)


def rope_tables(positions, width):
    half = width // 2
    index = jnp.arange(half).astype(f32)
    freq = jnp.power(rope_base, -(2.0 * index) / width)
    angle = positions.astype(f32)[..., None] * freq
    return (jnp.cos(angle), jnp.sin(angle))


def seq_positions(pairs, blk):
    count = pairs.shape[-1]
    offset = jnp.arange(2 * blk, dtype=jnp.int32)
    chosen = pairs[..., None]
    block = jnp.where(offset < blk, chosen, 2 * count - 1 - chosen)
    return block * blk + offset % blk


def after(x, *deps):
    return lax.optimization_barrier((x,) + deps)[0]


def unpack(where, mine, other, piece, outs):
    count = len(mine)

    def put(low, high):
        for i in range(count):
            block = where[i]
            start = 0
            for out in outs:
                size = out.shape[0] // count
                for at, ref in ((0, low[i]), (piece, high[i])):
                    lo, hi = max(start, at), min(start + size, at + piece)
                    if lo < hi:
                        to = pl.multiple_of(block * size + (lo - start), 16)
                        out[pl.ds(to, hi - lo), :] = ref[lo - at : hi - at, :]
                start += size

    @pl.when(where[count] == 0)
    def _():
        put(mine, other)

    @pl.when(where[count] != 0)
    def _():
        put(other, mine)


def qkv_kernel(count, heads, where, x, cosine, sine, *refs):
    mine, other = refs[:count], refs[count : 2 * count]
    wq, wk, wv, wo, gains, nin, qraw, kraw, qrot, kv = refs[2 * count :]
    piece = sum(w.shape[0] for w in (wq, wk, wv, wo)) // count // 2
    hd = wk.shape[0]
    unpack(where, mine, other, piece, (wq, wk, wv, wo))
    total = mine[0][piece:, :].astype(f32)
    for i in range(1, count):
        total = total + mine[i][piece:, :].astype(f32)
    gains[...] = total[: gains.shape[0], :]
    normed = norm(x[...].astype(f32), gains[0:1, :]).astype(bf)
    nin[...] = normed
    c, s = cosine[...], sine[...]
    half = hd // 2

    def turn(u):
        a, b = u[:, :half], u[:, half:]
        return a * c - b * s, b * c + a * s

    for h in range(heads):
        raw = times_t(normed, wq[h * hd : (h + 1) * hd, :])
        qraw[:, h * hd : (h + 1) * hd] = raw
        a, b = turn(norm(raw, gains[4:5, :hd]))
        qrot[:, h * hd : h * hd + half] = a.astype(bf)
        qrot[:, h * hd + half : (h + 1) * hd] = b.astype(bf)
    raw = times_t(normed, wk[...])
    kraw[...] = raw
    a, b = turn(norm(raw, gains[5:6, :hd]))
    kv[:, :half] = a.astype(bf)
    kv[:, half:hd] = b.astype(bf)
    kv[:, hd:] = times_t(normed, wv[...]).astype(bf)


def stacked(ref, rows, heads, hd):
    return jnp.concatenate([ref[rows, h * hd : (h + 1) * hd] for h in range(heads)], axis=0)


def attend_kernel(seqs, heads, scale, qpos, kpos, qrot, x, wo, gains, *refs):
    blocks = refs[:-6]
    att, probs, kall, proj, resid, nmid = refs[-6:]
    hd = kall.shape[1] // 2
    span = qrot.shape[0] // seqs
    length = len(blocks) * span
    for s in range(seqs):
        rows = slice(s * span, (s + 1) * span)
        for i, block in enumerate(blocks):
            kall[s * length + i * span : s * length + (i + 1) * span, :] = block[rows, :]
        keys = kall[s * length : (s + 1) * length, :hd]
        values = kall[s * length : (s + 1) * length, hd:]
        scores = times_t(stacked(qrot, rows, heads, hd), keys) * scale
        at = jnp.concatenate([qpos[rows, :]] * heads, axis=0)
        scores = jnp.where(kpos[s : s + 1, :] <= at, scores, -1e30)
        top = jnp.max(scores, axis=-1, keepdims=True)
        raised = jnp.exp(scores - top)
        p = raised / jnp.sum(raised, axis=-1, keepdims=True)
        probs[s * heads * span : (s + 1) * heads * span, :] = p
        out = times(p.astype(bf), values).astype(bf)
        for h in range(heads):
            att[rows, h * hd : (h + 1) * hd] = out[h * span : (h + 1) * span, :]
    projected = times(att[...], wo[...])
    proj[...] = projected
    r = x[...].astype(f32) + norm(projected, gains[1:2, :])
    resid[...] = r
    nmid[...] = norm(r, gains[2:3, :]).astype(bf)


def split(partial, count, keep, give):
    rows = partial.shape[0] // count
    for i in range(count):
        to = slice((i // 2) * rows, (i // 2 + 1) * rows)
        ref = give if i % 2 else keep
        ref[to, :] = partial[i * rows : (i + 1) * rows, :].astype(ref.dtype)


def ffn_kernel(count, members, *refs):
    chunks, blocks = refs[:count], refs[count : count + members]
    wg, wu, wd, nm, gate, up, hidden, keep, give = refs[count + members :]
    pc = wg.shape[0] // count
    rows = blocks[0].shape[0]
    for i in range(count):
        wg[i * pc : (i + 1) * pc, :] = chunks[i][:pc, :]
        wu[i * pc : (i + 1) * pc, :] = chunks[i][pc : 2 * pc, :]
        wd[i * pc : (i + 1) * pc, :] = chunks[i][2 * pc :, :]
    for i in range(members):
        nm[i * rows : (i + 1) * rows, :] = blocks[i][...]
    g = times_t(nm[...], wg[...])
    u = times_t(nm[...], wu[...])
    gate[...] = g
    up[...] = u
    t = jnp.tanh(root * (g + cubic * (g * g * g)))
    hid = (0.5 * g * (1.0 + t) * u).astype(bf)
    hidden[...] = hid
    split(times(hid, wd[...]), members, keep, give)


def ffn_end_kernel(keep, gave, resid, cot, gains, *refs):
    far, (out, d_ffn, dg) = refs[:-3], refs[-3:]
    rows = resid.shape[0]
    total = keep[:rows, :] + gave[:rows, :].astype(f32)
    for ref in far:
        total = total + ref[...].astype(f32)
    g = gains[3:4, :]
    out[...] = (resid[...] + norm(total, g)).astype(bf)
    d, dg[...] = norm_back(total, g, cot[...].astype(f32))
    d_ffn[...] = d.astype(bf)


def ffn_back_kernel(members, wg, wu, wd, gate, up, *refs):
    blocks = refs[:members]
    dall, dgate, dup, keep, give = refs[members:]
    rows = blocks[0].shape[0]
    for i in range(members):
        dall[i * rows : (i + 1) * rows, :] = blocks[i][...]
    d_hidden = times_t(dall[...], wd[...])
    g, u = gate[...], up[...]
    t = jnp.tanh(root * (g + cubic * (g * g * g)))
    slope = 0.5 * (1.0 + t) + 0.5 * g * (1.0 - t * t) * (root * (1.0 + 3.0 * cubic * (g * g)))
    dg = (d_hidden * u * slope).astype(bf)
    du = (d_hidden * (0.5 * g * (1.0 + t))).astype(bf)
    dgate[...] = dg
    dup[...] = du
    split(times(dg, wg[...]) + times(du, wu[...]), members, keep, give)


def ffn_grad_kernel(count, nm, dall, dgate, dup, hidden, keep, give):
    pc = hidden.shape[1] // count
    for k, (a, b) in enumerate(((dgate, nm), (dup, nm), (hidden, dall))):
        grad = t_times(a[...], b[...])
        for i in range(count):
            at = (i // 2) * 3 * pc + k * pc
            ref = give if i % 2 else keep
            ref[at : at + pc, :] = grad[i * pc : (i + 1) * pc, :].astype(ref.dtype)


def attend_back_kernel(seqs, heads, scale, keep, gave, resid, proj, cot, gains, wo, *refs):
    far = refs[:-11]
    probs, kall, qrot, d_resid, d_proj, dqrot, kkeep, kgive, dg_pf, dg_pa, dkall = refs[-11:]
    rows = resid.shape[0]
    hd = kall.shape[1] // 2
    span = rows // seqs
    length = kall.shape[0] // seqs
    total = keep[:rows, :] + gave[:rows, :].astype(f32)
    for ref in far:
        total = total + ref[...].astype(f32)
    d, dg_pf[...] = norm_back(resid[...], gains[2:3, :], total)
    d = d + cot[...].astype(f32)
    d_resid[...] = d
    d, dg_pa[...] = norm_back(proj[...], gains[1:2, :], d)
    d = d.astype(bf)
    d_proj[...] = d
    d_att = times_t(d, wo[...]).astype(bf)
    for s in range(seqs):
        at = slice(s * span, (s + 1) * span)
        keys = kall[s * length : (s + 1) * length, :hd]
        values = kall[s * length : (s + 1) * length, hd:]
        p = probs[s * heads * span : (s + 1) * heads * span, :]
        da = jnp.concatenate([d_att[at, h * hd : (h + 1) * hd] for h in range(heads)], axis=0)
        dp = times_t(da, values)
        delta = jnp.sum(p * dp, axis=-1, keepdims=True)
        ds = (p * (dp - delta) * scale).astype(bf)
        dq = times(ds, keys)
        for h in range(heads):
            dqrot[at, h * hd : (h + 1) * hd] = dq[h * span : (h + 1) * span, :]
        dkall[:, :hd] = t_times(ds, stacked(qrot, at, heads, hd))
        dkall[:, hd:] = t_times(p.astype(bf), da)
        for i in range(length // span):
            ref = kgive if i % 2 else kkeep
            to = (i // 2) * rows + s * span
            ref[to : to + span, :] = dkall[i * span : (i + 1) * span, :].astype(ref.dtype)


def unturn(d, c, s):
    half = d.shape[1] // 2
    a, b = d[:, :half], d[:, half:]
    return jnp.concatenate([a * c + b * s, b * c - a * s], axis=1)


def packed(count, where, sources, keep, give, tail=None):
    twin = where[count]
    sizes = [src.shape[0] // count // 2 for src in sources]
    each = sum(sizes)
    for i in range(count):
        block = where[i]
        to = ((i % 2) * (count // 2) + i // 2) * each
        for src, size in zip(sources, sizes):
            own = pl.multiple_of(block * (2 * size) + twin * size, 8)
            their = pl.multiple_of(block * (2 * size) + (1 - twin) * size, 8)
            keep[to : to + size, :] = src[pl.ds(own, size), :].astype(keep.dtype)
            give[to : to + size, :] = src[pl.ds(their, size), :].astype(bf)
            to += size
    if tail is not None:
        keep[count * each :, :] = tail.astype(keep.dtype)
        give[count * each :, :] = tail.astype(bf)


def query_back_kernel(
    count, heads, where, dqrot, qraw, gains, cosine, sine, nin, att, d_proj, dq, dg_q, keep, give, gq, go
):
    hd = qraw.shape[1] // heads
    c, s = cosine[...], sine[...]
    total = jnp.zeros((1, hd), f32)
    for h in range(heads):
        at = slice(h * hd, (h + 1) * hd)
        d, dg = norm_back(qraw[:, at], gains[4:5, :hd], unturn(dqrot[:, at], c, s))
        dq[:, at] = d.astype(bf)
        total = total + dg
    dg_q[...] = total
    gq[...] = t_times(dq[...], nin[...])
    go[...] = t_times(att[...], d_proj[...])
    packed(count, where, (gq, go), keep, give)


def key_back_kernel(
    count, where, kkeep, kgave, kraw, gains, cosine, sine, nin, dq, wq, wk, wv, x, d_resid, dg_po, dg_pf, dg_pa, dg_q, *refs
):
    far, (grad, keep, give, gk, gv) = refs[:-5], refs[-5:]
    rows, hd = kraw.shape
    total = kkeep[:rows, :] + kgave[:rows, :].astype(f32)
    for ref in far:
        total = total + ref[...].astype(f32)
    d, dg_k = norm_back(
        kraw[...], gains[5:6, :hd], unturn(total[:, :hd], cosine[...], sine[...])
    )
    dk = d.astype(bf)
    dv = total[:, hd:].astype(bf)
    d_in = times(dq[...], wq[...]) + times(dk, wk[...]) + times(dv, wv[...])
    d, dg_in = norm_back(x[...].astype(f32), gains[0:1, :], d_in)
    grad[...] = d_resid[...] + d
    gk[...] = t_times(dk, nin[...])
    gv[...] = t_times(dv, nin[...])
    pad = jnp.zeros((1, nin.shape[1] - hd), f32)
    none = jnp.zeros((2, nin.shape[1]), f32)
    tail = jnp.concatenate(
        [
            dg_in,
            dg_pa[...],
            dg_pf[...],
            dg_po[...],
            jnp.concatenate([dg_q[...], pad], axis=1),
            jnp.concatenate([dg_k, pad], axis=1),
            none,
        ],
        axis=0,
    )
    packed(count, where, (gk, gv), keep, give, tail)


def near_kernel(half, keep, gave, keep2, give2):
    tail = keep.shape[0] - 2 * half
    keep2[:half, :] = keep[:half, :].astype(f32) + gave[:half, :].astype(f32)
    rest = slice(half, 2 * half)
    give2[:half, :] = (keep[rest, :].astype(f32) + gave[rest, :].astype(f32)).astype(bf)
    if tail:
        t = keep[2 * half :, :].astype(f32) + gave[2 * half :, :].astype(f32)
        keep2[half:, :] = t
        give2[half:, :] = t.astype(bf)


def part_kernel(parts, blocks, outer, keep, gave, own, *gives):
    rows = keep.shape[0] // blocks
    size = rows // parts
    for a, out in enumerate((own, *gives)):
        part = lax.rem(outer[0] + a, parts)
        for i in range(blocks):
            at = pl.ds(pl.multiple_of(i * rows + part * size, 8), size)
            total = keep[at, :].astype(f32) + gave[at, :].astype(f32)
            out[i * size : (i + 1) * size, :] = total.astype(out.dtype)


def far_kernel(parts, rows, keep, gave, *outs):
    tail = keep.shape[0] - parts * rows
    for a in range(parts):
        at = slice(a * rows, (a + 1) * rows)
        outs[a][:rows, :] = (keep[at, :].astype(f32) + gave[at, :].astype(f32)).astype(outs[a].dtype)
    if tail:
        at = slice(parts * rows, parts * rows + tail)
        t = keep[at, :].astype(f32) + gave[at, :].astype(f32)
        for a in range(parts):
            outs[a][rows:, :] = t.astype(outs[a].dtype)


def ffn_out_kernel(members, where, *refs):
    blocks, (gate, up, down, buf) = refs[:members], refs[members:]
    pc = blocks[0].shape[0] // 3
    for k, out in enumerate((gate, up, down)):
        to_ref = out if k == 2 else buf
        for i in range(members):
            to = pl.multiple_of(where[i] * pc, 8)
            to_ref[pl.ds(to, pc), :] = blocks[i][k * pc : (k + 1) * pc, :].astype(f32)
        if k < 2:
            out[...] = buf[...].T


def joined(sizes, twin, mine, other, outs):
    def put(low, high):
        start = 0
        for size, out in zip(sizes, outs):
            half = size // 2
            rows = slice(start, start + half)
            start += half
            out[:half, :] = low[rows, :].astype(f32)
            out[half:, :] = high[rows, :].astype(f32)

    @pl.when(twin == 0)
    def _():
        put(mine, other)

    @pl.when(twin != 0)
    def _():
        put(other, mine)


def query_out_kernel(sizes, where, *refs):
    blocks, (out_q, out_o, buf) = refs[:-3], refs[-3:]
    size = blocks[0].shape[0]
    half = buf.shape[0] // 2
    for i, block in enumerate(blocks):
        to = pl.multiple_of(lax.rem(where[i], 2) * half + where[i] // 2 * size, 8)
        buf[pl.ds(to, size), :] = block[...].astype(f32)
    low, high = sizes[0] // 2, sizes[1] // 2
    out_q[...] = jnp.concatenate([buf[:low, :], buf[half : half + low, :]], axis=0).T
    out_o[:high, :] = buf[low:half, :]
    out_o[high:, :] = buf[half + low :, :]


def key_out_kernel(sizes, at, mine, other, out_k, out_v, *gains):
    joined(sizes, at[0], mine, other, (out_k, out_v))
    tail = mine[mine.shape[0] - 8 :, :]
    for first, last in ((0, 4), (4, 6)):
        size = gains[first].shape[0]
        shape = (tail.shape[1], size)
        row = lax.broadcasted_iota(jnp.int32, shape, 0)
        col = lax.broadcasted_iota(jnp.int32, shape, 1)
        own = times(tail, (row == at[1] * size + col).astype(f32).astype(bf))
        for i in range(first, last):
            gains[i][...] = own[i, :]


def shards(
    layer_input,
    out_cotangent,
    block_pairs,
    w_query,
    w_key,
    w_value,
    w_output,
    w_gate,
    w_up,
    w_down,
    input_gain,
    attnpost_gain,
    ffnpre_gain,
    ffnpost_gain,
    query_gain,
    key_gain,
):
    S, C = Axis("shard"), Axis("ctx")
    seqs, span, width = layer_input.shape
    rows = seqs * span
    members, count = C.size, S.size
    twin = C.rank % 2
    pq, pk, po, pf = w_query.shape[1], w_key.shape[1], w_output.shape[0], w_down.shape[0]
    hd = query_gain.shape[0] * count
    hq = pq * count
    heads = hq // hd
    scale = hd ** (-0.5)
    where = jnp.stack(S.sources() + [twin]).astype(jnp.int32)
    members_from = jnp.stack(C.sources()).astype(jnp.int32)
    x = layer_input.reshape(rows, width)
    cot = out_cotangent.reshape(rows, width)

    small = [input_gain, attnpost_gain, ffnpre_gain, ffnpost_gain, query_gain, key_gain]

    def placed(same):
        size = same[0].shape[0]
        at = jnp.arange(width)[None, :] == S.rank * size + jnp.arange(size)[:, None]
        return times(jnp.stack(same), at.astype(bf)).astype(bf)

    gain_rows = jnp.concatenate([placed(small[:4]), placed(small[4:])], axis=0)
    gain_rows = jnp.pad(gain_rows, ((0, 8 - len(small)), (0, 0)))

    whole = jnp.concatenate([w_query.T, w_key.T, w_value.T, w_output], axis=0)
    piece = whole.shape[0] // 2
    own = jnp.where(twin == 0, whole[:piece], whole[piece:])
    first = jnp.concatenate([own, gain_rows], axis=0)
    mine = S.gather(first)
    other = [C.send(m, 0, 1) for m in mine]

    pc = pf // members

    def part_of(w):
        return lax.dynamic_slice_in_dim(w, C.rank * pc, pc, 0)

    ffn = jnp.concatenate([part_of(w_gate.T), part_of(w_up.T), part_of(w_down)], axis=0)
    chunks = S.gather(after(ffn, *mine[2::2]))

    places = seq_positions(block_pairs, span // 2)
    kpos = jnp.concatenate(
        [lax.dynamic_index_in_dim(places, o, 1, keepdims=False) for o in C.sources()], axis=1
    )
    own_pos = lax.dynamic_index_in_dim(places, C.rank, 1, keepdims=False).reshape(rows)
    cosine, sine = rope_tables(own_pos, hd)
    qpos = own_pos[:, None]
    key_at = jnp.stack([twin, S.rank]).astype(jnp.int32)
    x, qpos, kpos, members_from, key_at = lax.optimization_barrier(
        (x, qpos, kpos, members_from, key_at)
    )

    wq, wk, wv, wo, gains, nin, qraw, kraw, qrot, kv = call(
        functools.partial(qkv_kernel, count, heads),
        [
            ((hq, width), bf),
            ((hd, width), bf),
            ((hd, width), bf),
            ((hq, width), bf),
            ((8, width), f32),
            ((rows, width), bf),
            ((rows, hq), f32),
            ((rows, hd), f32),
            ((rows, hq), bf),
            ((rows, 2 * hd), bf),
        ],
        (where, x, cosine, sine, *mine, *other),
        scalars=1,
    )
    kvs = C.gather(kv)
    length = members * span
    att, probs, kall, proj, resid, nmid = call(
        functools.partial(attend_kernel, seqs, heads, scale),
        [
            ((rows, hq), bf),
            ((seqs * heads * span, length), f32),
            ((seqs * length, 2 * hd), bf),
            ((rows, width), f32),
            ((rows, width), f32),
            ((rows, width), bf),
        ],
        (qpos, kpos, qrot, x, wo, gains, *kvs),
    )
    hid = count * pc
    wg, wu, wd, nm, gate, up, hidden, keep, give = call(
        functools.partial(ffn_kernel, count, members),
        [
            ((hid, width), bf),
            ((hid, width), bf),
            ((hid, width), bf),
            ((members * rows, width), bf),
            ((members * rows, hid), f32),
            ((members * rows, hid), f32),
            ((members * rows, hid), bf),
            ((C.outer * rows, width), f32),
            ((C.outer * rows, width), bf),
        ],
        (*chunks, *C.gather(nmid)),
    )

    def home(keep, give):
        gave = C.send(give, 0, 1)
        far = []
        for a in range(1, C.outer):
            at = slice(a * rows, (a + 1) * rows)
            part = (keep[at] + gave[at].astype(f32)).astype(bf)
            far.append(C.send(part, C.outer - a, 0))
        return gave, far

    gave, far = home(keep, give)
    layer_output, d_ffn, dg_po = call(
        ffn_end_kernel,
        [((rows, width), bf), ((rows, width), bf), ((1, width), f32)],
        (keep, gave, resid, cot, gains, *far),
    )
    dall, dgate, dup, keep, give = call(
        functools.partial(ffn_back_kernel, members),
        [
            ((members * rows, width), bf),
            ((members * rows, hid), bf),
            ((members * rows, hid), bf),
            ((C.outer * rows, width), f32),
            ((C.outer * rows, width), bf),
        ],
        (wg, wu, wd, gate, up, *C.gather(d_ffn)),
    )
    gave, far = home(keep, give)

    def spread(keep, give, each):
        got = S.send(give, 0, 1)
        n = each + keep.shape[0] - S.outer * each
        parts = call(
            functools.partial(far_kernel, S.outer, each),
            [((n, width), f32)] + [((n, width), bf)] * (S.outer - 1),
            (keep, got),
        )
        return [parts[0]] + [S.send(parts[a], S.outer - a, 0) for a in range(1, S.outer)]

    def summed(terms):
        total = terms[0].astype(f32)
        for term in terms[1:]:
            total = total + term.astype(f32)
        return total.astype(bf)

    fkeep, fgive = call(
        functools.partial(ffn_grad_kernel, count),
        [((S.outer * 3 * pc, width), bf), ((S.outer * 3 * pc, width), bf)],
        (nm, dall, dgate, dup, hidden),
    )
    f_terms = spread(fkeep, fgive, 3 * pc)

    d_resid, d_proj, dqrot, kkeep, kgive, dg_pf, dg_pa = call(
        functools.partial(attend_back_kernel, seqs, heads, scale),
        [
            ((rows, width), f32),
            ((rows, width), bf),
            ((rows, hq), f32),
            ((C.outer * rows, 2 * hd), f32),
            ((C.outer * rows, 2 * hd), bf),
            ((1, width), f32),
            ((1, width), f32),
        ],
        (keep, gave, resid, proj, cot, gains, wo, *far, probs, kall, qrot),
        scratch=[pltpu.VMEM((length, 2 * hd), f32)],
    )
    kgave, kfar = home(kkeep, kgive)

    def begin(keep, give, each):
        got = C.send(give, 0, 1)
        half = S.outer * each
        n = keep.shape[0] - half
        keep, give = call(
            functools.partial(near_kernel, half), [((n, width), f32), ((n, width), bf)], (keep, got)
        )
        return spread(keep, give, each)

    def finish(terms):
        part = summed(terms)
        far = [C.send(part, a, 0) for a in range(1, C.outer)]
        total = summed([part] + far)
        return total, C.send(total, 0, 1)

    each_q, each_k = (pq + po) // 2, pk
    dq, dg_q, keep, give = call(
        functools.partial(query_back_kernel, count, heads),
        [
            ((rows, hq), bf),
            ((1, hd), f32),
            ((count * each_q, width), bf),
            ((count * each_q, width), bf),
        ],
        (where, dqrot, qraw, gains, cosine, sine, nin, att, d_proj),
        scalars=1,
        scratch=[pltpu.VMEM((hq, width), f32), pltpu.VMEM((hq, width), f32)],
    )
    q_got = C.send(give, 0, 1)
    each_q //= C.outer
    q_own, *q_gives = call(
        functools.partial(part_kernel, C.outer, count),
        [((count * each_q, width), f32)] + [((count * each_q, width), bf)] * (C.outer - 1),
        ((C.rank // 2).astype(jnp.int32)[None], keep, q_got),
        scalars=1,
    )
    for a, give in enumerate(q_gives):
        q_own = q_own + C.send(give, a + 1, 0).astype(f32)
    half = S.outer * each_q
    q_terms = spread(q_own[:half], q_own[half:].astype(bf), each_q)
    input_grad, keep, give = call(
        functools.partial(key_back_kernel, count),
        [
            ((rows, width), f32),
            ((count * each_k + 8, width), f32),
            ((count * each_k + 8, width), bf),
        ],
        (
            where,
            kkeep,
            kgave,
            kraw,
            gains,
            cosine,
            sine,
            nin,
            dq,
            wq,
            wk,
            wv,
            x,
            d_resid,
            dg_po,
            dg_pf,
            dg_pa,
            dg_q,
            *kfar,
        ),
        scalars=1,
        scratch=[pltpu.VMEM((hd, width), f32), pltpu.VMEM((hd, width), f32)],
    )
    k_terms = begin(keep, give, each_k)
    all_q = C.gather(summed(q_terms))
    total_k = finish(k_terms)

    out_gate, out_up, out_down = call(
        functools.partial(ffn_out_kernel, members),
        [((width, pf), f32), ((width, pf), f32), ((pf, width), f32)],
        (members_from, *C.gather(summed(f_terms))),
        scalars=1,
        scratch=[pltpu.VMEM((pf, width), f32)],
    )
    out_query, out_output = call(
        functools.partial(query_out_kernel, (pq, po)),
        [((width, pq), f32), ((po, width), f32)],
        (members_from, *all_q),
        scalars=1,
        scratch=[pltpu.VMEM((pq + po, width), f32)],
    )
    out_key, out_value, *sums = call(
        functools.partial(key_out_kernel, (pk, pk)),
        [((pk, width), f32), ((pk, width), f32)] + [(g.shape, f32) for g in small],
        (key_at, *total_k),
        scalars=1,
    )
    out_key, out_value = out_key.T, out_value.T
    return (
        layer_output.reshape(seqs, span, width),
        input_grad.reshape(seqs, span, width),
        out_query,
        out_key,
        out_value,
        out_output,
        out_gate,
        out_up,
        out_down,
        *sums,
    )


def solution(mesh):
    lead2 = P("shard", "ctx", None)
    cols = P(None, "shard")
    lead = P("shard", None)
    gain = P("shard")
    return jax.shard_map(
        shards,
        mesh=mesh,
        in_specs=(lead2, lead2, lead, cols, cols, cols, lead, cols, cols, lead) + (gain,) * 6,
        out_specs=(lead2, lead2, cols, cols, cols, lead, cols, cols, lead) + (gain,) * 6,
        check_vma=False,
    )
```

```python
import functools

import jax
import jax.numpy as jnp
from jax import lax
from jax.experimental import pallas as pl
from jax.experimental.pallas import tpu as pltpu
from jax.sharding import PartitionSpec as P


epsilon = 1e-06
rope_base = 1000000.0
bf = jnp.bfloat16
f32 = jnp.float32
root = 0.7978845608028654
cubic = 0.044715


class Axis:
    def __init__(self, name):
        self.name = name
        self.size = lax.axis_size(name)
        assert self.size % 2 == 0
        self.inner = 2
        self.outer = self.size // 2
        self.rank = lax.axis_index(name)

    def send(self, x, d_outer, d_inner):
        n, m = self.outer, self.inner
        pairs = [
            (i, ((i // m + d_outer) % n) * m + (i % m + d_inner) % m) for i in range(self.size)
        ]
        return lax.ppermute(x, self.name, pairs)

    def shifts(self):
        return [(a, b) for a in range(self.outer) for b in range(self.inner)]

    def sources(self):
        n, m = self.outer, self.inner
        return [
            ((self.rank // m + n - a) % n) * m + (self.rank % m + m - b) % m
            for a, b in self.shifts()
        ]

    def gather(self, x):
        out = []
        for a in range(self.outer):
            far = self.send(x, a, 0) if a else x
            out += [far, self.send(far, 0, 1)]
        return out


def times(a, b):
    return lax.dot_general(a, b, (((1,), (0,)), ((), ())), preferred_element_type=f32)


def times_t(a, b):
    return lax.dot_general(a, b, (((1,), (1,)), ((), ())), preferred_element_type=f32)


def t_times(a, b):
    return lax.dot_general(a, b, (((0,), (0,)), ((), ())), preferred_element_type=f32)


def inverse_rms(v):
    return lax.rsqrt(jnp.mean(v * v, axis=-1, keepdims=True) + epsilon)


def norm(v, g):
    return v * inverse_rms(v) * g


def norm_back(v, g, dy):
    r = inverse_rms(v)
    gd = g * dy
    dv = r * gd - v * (r * r * r) * jnp.mean(v * gd, axis=-1, keepdims=True)
    return dv, jnp.sum(dy * v * r, axis=0, keepdims=True)


def call(body, outs, args, scalars=0, scratch=()):
    vmem = pl.BlockSpec(memory_space=pltpu.VMEM)
    smem = pl.BlockSpec(memory_space=pltpu.SMEM)
    return pl.pallas_call(
        body,
        out_shape=[jax.ShapeDtypeStruct(shape, kind) for shape, kind in outs],
        in_specs=[smem] * scalars + [vmem] * (len(args) - scalars),
        out_specs=[vmem] * len(outs),
        scratch_shapes=list(scratch),
    )(*args)


def rope_tables(positions, width):
    half = width // 2
    index = jnp.arange(half).astype(f32)
    freq = jnp.power(rope_base, -(2.0 * index) / width)
    angle = positions.astype(f32)[..., None] * freq
    return (jnp.cos(angle), jnp.sin(angle))


def seq_positions(pairs, blk):
    count = pairs.shape[-1]
    offset = jnp.arange(2 * blk, dtype=jnp.int32)
    chosen = pairs[..., None]
    block = jnp.where(offset < blk, chosen, 2 * count - 1 - chosen)
    return block * blk + offset % blk


def after(x, *deps):
    return lax.optimization_barrier((x,) + deps)[0]


def unpack(where, mine, other, piece, outs, start=0):
    count = len(mine)
    first = start

    def put(low, high):
        for i in range(count):
            block = where[i]
            start = first
            for out in outs:
                size = out.shape[0] // count
                for at, ref in ((0, low[i]), (piece, high[i])):
                    lo, hi = max(start, at), min(start + size, at + piece)
                    if lo < hi:
                        to = pl.multiple_of(block * size + (lo - start), 16)
                        out[pl.ds(to, hi - lo), :] = ref[lo - at : hi - at, :]
                start += size

    @pl.when(where[count] == 0)
    def _():
        put(mine, other)

    @pl.when(where[count] != 0)
    def _():
        put(other, mine)


def qkv_kernel(count, heads, where, x, cosine, sine, *refs):
    mine, other = refs[:count], refs[count : 2 * count]
    wq, wk, wv, gains, nin, qraw, kraw, qrot, kv = refs[2 * count :]
    piece = mine[0].shape[0] - 8
    hd = wk.shape[0]
    unpack(where, mine, other, piece, (wq, wk, wv))
    total = mine[0][piece:, :].astype(f32)
    for i in range(1, count):
        total = total + mine[i][piece:, :].astype(f32)
    gains[...] = total[: gains.shape[0], :]
    normed = norm(x[...].astype(f32), gains[0:1, :]).astype(bf)
    nin[...] = normed
    c, s = cosine[...], sine[...]
    half = hd // 2

    def turn(u):
        a, b = u[:, :half], u[:, half:]
        return a * c - b * s, b * c + a * s

    for h in range(heads):
        raw = times_t(normed, wq[h * hd : (h + 1) * hd, :])
        qraw[:, h * hd : (h + 1) * hd] = raw
        a, b = turn(norm(raw, gains[4:5, :hd]))
        qrot[:, h * hd : h * hd + half] = a.astype(bf)
        qrot[:, h * hd + half : (h + 1) * hd] = b.astype(bf)
    raw = times_t(normed, wk[...])
    kraw[...] = raw
    a, b = turn(norm(raw, gains[5:6, :hd]))
    kv[:, :half] = a.astype(bf)
    kv[:, half:hd] = b.astype(bf)
    kv[:, hd:] = times_t(normed, wv[...]).astype(bf)


def output_weight_kernel(count, start, where, *refs):
    mine, other = refs[:count], refs[count : 2 * count]
    unpack(where, mine, other, mine[0].shape[0] - 8, refs[2 * count :], start)


def stacked(ref, rows, heads, hd):
    return jnp.concatenate([ref[rows, h * hd : (h + 1) * hd] for h in range(heads)], axis=0)


def attend_kernel(seqs, heads, scale, qpos, kpos, qrot, x, wo, gains, *refs):
    blocks = refs[:-6]
    att, probs, kall, proj, resid, nmid = refs[-6:]
    hd = kall.shape[1] // 2
    span = qrot.shape[0] // seqs
    length = len(blocks) * span
    for s in range(seqs):
        rows = slice(s * span, (s + 1) * span)
        for i, block in enumerate(blocks):
            kall[s * length + i * span : s * length + (i + 1) * span, :] = block[rows, :]
        keys = kall[s * length : (s + 1) * length, :hd]
        values = kall[s * length : (s + 1) * length, hd:]
        scores = times_t(stacked(qrot, rows, heads, hd), keys) * scale
        at = jnp.concatenate([qpos[rows, :]] * heads, axis=0)
        scores = jnp.where(kpos[s : s + 1, :] <= at, scores, -1e30)
        top = jnp.max(scores, axis=-1, keepdims=True)
        raised = jnp.exp(scores - top)
        p = raised / jnp.sum(raised, axis=-1, keepdims=True)
        probs[s * heads * span : (s + 1) * heads * span, :] = p
        out = times(p.astype(bf), values).astype(bf)
        for h in range(heads):
            att[rows, h * hd : (h + 1) * hd] = out[h * span : (h + 1) * span, :]
    projected = times(att[...], wo[...])
    proj[...] = projected
    r = x[...].astype(f32) + norm(projected, gains[1:2, :])
    resid[...] = r
    nmid[...] = norm(r, gains[2:3, :]).astype(bf)


def split(partial, count, keep, give):
    rows = partial.shape[0] // count
    for i in range(count):
        to = slice((i // 2) * rows, (i // 2 + 1) * rows)
        ref = give if i % 2 else keep
        ref[to, :] = partial[i * rows : (i + 1) * rows, :].astype(ref.dtype)


def ffn_kernel(count, members, *refs):
    chunks, blocks = refs[:count], refs[count : count + members]
    wg, wu, wd, nm, gate, up, hidden, keep, give = refs[count + members :]
    pc = wg.shape[0] // count
    rows = blocks[0].shape[0]
    for i in range(count):
        wg[i * pc : (i + 1) * pc, :] = chunks[i][:pc, :]
        wu[i * pc : (i + 1) * pc, :] = chunks[i][pc : 2 * pc, :]
        wd[i * pc : (i + 1) * pc, :] = chunks[i][2 * pc :, :]
    for i in range(members):
        nm[i * rows : (i + 1) * rows, :] = blocks[i][...]
    g = times_t(nm[...], wg[...])
    u = times_t(nm[...], wu[...])
    gate[...] = g.astype(bf)
    up[...] = u.astype(bf)
    t = jnp.tanh(root * (g + cubic * (g * g * g)))
    hid = (0.5 * g * (1.0 + t) * u).astype(bf)
    hidden[...] = hid
    split(times(hid, wd[...]), members, keep, give)


def ffn_end_kernel(keep, gave, resid, cot, gains, *refs):
    far, (out, d_ffn, dg) = refs[:-3], refs[-3:]
    rows = resid.shape[0]
    total = keep[:rows, :] + gave[:rows, :].astype(f32)
    for ref in far:
        total = total + ref[...].astype(f32)
    g = gains[3:4, :]
    out[...] = (resid[...] + norm(total, g)).astype(bf)
    d, dg[...] = norm_back(total, g, cot[...].astype(f32))
    d_ffn[...] = d.astype(bf)


def ffn_back_kernel(members, wg, wu, wd, gate, up, *refs):
    blocks = refs[:members]
    dall, dgate, dup, keep, give = refs[members:]
    rows = blocks[0].shape[0]
    for i in range(members):
        dall[i * rows : (i + 1) * rows, :] = blocks[i][...]
    d_hidden = times_t(dall[...], wd[...])
    g, u = gate[...].astype(f32), up[...].astype(f32)
    t = jnp.tanh(root * (g + cubic * (g * g * g)))
    slope = 0.5 * (1.0 + t) + 0.5 * g * (1.0 - t * t) * (root * (1.0 + 3.0 * cubic * (g * g)))
    dg = (d_hidden * u * slope).astype(bf)
    du = (d_hidden * (0.5 * g * (1.0 + t))).astype(bf)
    dgate[...] = dg
    dup[...] = du
    split(times(dg, wg[...]) + times(du, wu[...]), members, keep, give)


def ffn_grad_kernel(count, nm, dall, dgate, dup, hidden, keep, give):
    pc = hidden.shape[1] // count
    for k, (a, b) in enumerate(((dgate, nm), (dup, nm), (hidden, dall))):
        grad = t_times(a[...], b[...])
        for i in range(count):
            at = (i // 2) * 3 * pc + k * pc
            ref = give if i % 2 else keep
            ref[at : at + pc, :] = grad[i * pc : (i + 1) * pc, :].astype(ref.dtype)


def attend_back_kernel(seqs, heads, scale, keep, gave, resid, proj, cot, gains, wo, *refs):
    far = refs[:-11]
    probs, kall, qrot, d_resid, d_proj, dqrot, kkeep, kgive, dg_pf, dg_pa, dkall = refs[-11:]
    rows = resid.shape[0]
    hd = kall.shape[1] // 2
    span = rows // seqs
    length = kall.shape[0] // seqs
    total = keep[:rows, :] + gave[:rows, :].astype(f32)
    for ref in far:
        total = total + ref[...].astype(f32)
    d, dg_pf[...] = norm_back(resid[...], gains[2:3, :], total)
    d = d + cot[...].astype(f32)
    d_resid[...] = d
    d, dg_pa[...] = norm_back(proj[...], gains[1:2, :], d)
    d = d.astype(bf)
    d_proj[...] = d
    d_att = times_t(d, wo[...]).astype(bf)
    for s in range(seqs):
        at = slice(s * span, (s + 1) * span)
        keys = kall[s * length : (s + 1) * length, :hd]
        values = kall[s * length : (s + 1) * length, hd:]
        p = probs[s * heads * span : (s + 1) * heads * span, :]
        da = jnp.concatenate([d_att[at, h * hd : (h + 1) * hd] for h in range(heads)], axis=0)
        dp = times_t(da, values)
        delta = jnp.sum(p * dp, axis=-1, keepdims=True)
        ds = (p * (dp - delta) * scale).astype(bf)
        dq = times(ds, keys)
        for h in range(heads):
            dqrot[at, h * hd : (h + 1) * hd] = dq[h * span : (h + 1) * span, :]
        dkall[:, :hd] = t_times(ds, stacked(qrot, at, heads, hd))
        dkall[:, hd:] = t_times(p.astype(bf), da)
        for i in range(length // span):
            ref = kgive if i % 2 else kkeep
            to = (i // 2) * rows + s * span
            ref[to : to + span, :] = dkall[i * span : (i + 1) * span, :].astype(ref.dtype)


def unturn(d, c, s):
    half = d.shape[1] // 2
    a, b = d[:, :half], d[:, half:]
    return jnp.concatenate([a * c + b * s, b * c - a * s], axis=1)


def packed(count, where, sources, keep, give, tail=None):
    twin = where[count]
    sizes = [src.shape[0] // count // 2 for src in sources]
    each = sum(sizes)
    for i in range(count):
        block = where[i]
        to = ((i % 2) * (count // 2) + i // 2) * each
        for src, size in zip(sources, sizes):
            own = pl.multiple_of(block * (2 * size) + twin * size, 8)
            their = pl.multiple_of(block * (2 * size) + (1 - twin) * size, 8)
            keep[to : to + size, :] = src[pl.ds(own, size), :].astype(keep.dtype)
            give[to : to + size, :] = src[pl.ds(their, size), :].astype(bf)
            to += size
    if tail is not None:
        keep[count * each :, :] = tail.astype(keep.dtype)
        give[count * each :, :] = tail.astype(bf)


def query_back_kernel(
    count, heads, where, dqrot, qraw, gains, cosine, sine, nin, att, d_proj, dq, dg_q, keep, give, gq, go
):
    hd = qraw.shape[1] // heads
    c, s = cosine[...], sine[...]
    total = jnp.zeros((1, hd), f32)
    for h in range(heads):
        at = slice(h * hd, (h + 1) * hd)
        d, dg = norm_back(qraw[:, at], gains[4:5, :hd], unturn(dqrot[:, at], c, s))
        dq[:, at] = d.astype(bf)
        total = total + dg
    dg_q[...] = total
    gq[...] = t_times(dq[...], nin[...])
    go[...] = t_times(att[...], d_proj[...])
    packed(count, where, (gq, go), keep, give)


def key_back_kernel(
    count, where, kkeep, kgave, kraw, gains, cosine, sine, nin, dq, wq, wk, wv, x, d_resid, dg_po, dg_pf, dg_pa, dg_q, *refs
):
    far, (grad, keep, give, gk, gv) = refs[:-5], refs[-5:]
    rows, hd = kraw.shape
    total = kkeep[:rows, :] + kgave[:rows, :].astype(f32)
    for ref in far:
        total = total + ref[...].astype(f32)
    d, dg_k = norm_back(
        kraw[...], gains[5:6, :hd], unturn(total[:, :hd], cosine[...], sine[...])
    )
    dk = d.astype(bf)
    dv = total[:, hd:].astype(bf)
    d_in = times(dq[...], wq[...]) + times(dk, wk[...]) + times(dv, wv[...])
    d, dg_in = norm_back(x[...].astype(f32), gains[0:1, :], d_in)
    grad[...] = d_resid[...] + d
    gk[...] = t_times(dk, nin[...])
    gv[...] = t_times(dv, nin[...])
    pad = jnp.zeros((1, nin.shape[1] - hd), f32)
    none = jnp.zeros((2, nin.shape[1]), f32)
    tail = jnp.concatenate(
        [
            dg_in,
            dg_pa[...],
            dg_pf[...],
            dg_po[...],
            jnp.concatenate([dg_q[...], pad], axis=1),
            jnp.concatenate([dg_k, pad], axis=1),
            none,
        ],
        axis=0,
    )
    packed(count, where, (gk, gv), keep, give, tail)


def near_kernel(half, keep, gave, keep2, give2):
    tail = keep.shape[0] - 2 * half
    keep2[:half, :] = keep[:half, :].astype(f32) + gave[:half, :].astype(f32)
    rest = slice(half, 2 * half)
    give2[:half, :] = (keep[rest, :].astype(f32) + gave[rest, :].astype(f32)).astype(bf)
    if tail:
        t = keep[2 * half :, :].astype(f32) + gave[2 * half :, :].astype(f32)
        keep2[half:, :] = t
        give2[half:, :] = t.astype(bf)


def part_kernel(parts, blocks, outer, keep, gave, own, *gives):
    rows = keep.shape[0] // blocks
    size = rows // parts
    for a, out in enumerate((own, *gives)):
        part = lax.rem(outer[0] + a, parts)
        for i in range(blocks):
            at = pl.ds(pl.multiple_of(i * rows + part * size, 8), size)
            total = keep[at, :].astype(f32) + gave[at, :].astype(f32)
            out[i * size : (i + 1) * size, :] = total.astype(out.dtype)


def far_kernel(parts, rows, keep, gave, *outs):
    tail = keep.shape[0] - parts * rows
    for a in range(parts):
        at = slice(a * rows, (a + 1) * rows)
        outs[a][:rows, :] = (keep[at, :].astype(f32) + gave[at, :].astype(f32)).astype(outs[a].dtype)
    if tail:
        at = slice(parts * rows, parts * rows + tail)
        t = keep[at, :].astype(f32) + gave[at, :].astype(f32)
        for a in range(parts):
            outs[a][rows:, :] = t.astype(outs[a].dtype)


def ffn_out_kernel(members, where, *refs):
    blocks, (gate, up, down, buf) = refs[:members], refs[members:]
    pc = blocks[0].shape[0] // 3
    for k, out in enumerate((gate, up, down)):
        to_ref = out if k == 2 else buf
        for i in range(members):
            to = pl.multiple_of(where[i] * pc, 8)
            to_ref[pl.ds(to, pc), :] = blocks[i][k * pc : (k + 1) * pc, :].astype(f32)
        if k < 2:
            out[...] = buf[...].T


def joined(sizes, twin, mine, other, outs):
    def put(low, high):
        start = 0
        for size, out in zip(sizes, outs):
            half = size // 2
            rows = slice(start, start + half)
            start += half
            out[:half, :] = low[rows, :].astype(f32)
            out[half:, :] = high[rows, :].astype(f32)

    @pl.when(twin == 0)
    def _():
        put(mine, other)

    @pl.when(twin != 0)
    def _():
        put(other, mine)


def query_out_kernel(sizes, where, *refs):
    blocks, (out_q, out_o, buf) = refs[:-3], refs[-3:]
    size = blocks[0].shape[0]
    half = buf.shape[0] // 2
    for i, block in enumerate(blocks):
        to = pl.multiple_of(lax.rem(where[i], 2) * half + where[i] // 2 * size, 8)
        buf[pl.ds(to, size), :] = block[...].astype(f32)
    low, high = sizes[0] // 2, sizes[1] // 2
    out_q[...] = jnp.concatenate([buf[:low, :], buf[half : half + low, :]], axis=0).T
    out_o[:high, :] = buf[low:half, :]
    out_o[high:, :] = buf[half + low :, :]


def key_out_kernel(sizes, at, mine, other, out_k, out_v, *gains):
    joined(sizes, at[0], mine, other, (out_k, out_v))
    tail = mine[mine.shape[0] - 8 :, :]
    for first, last in ((0, 4), (4, 6)):
        size = gains[first].shape[0]
        shape = (tail.shape[1], size)
        row = lax.broadcasted_iota(jnp.int32, shape, 0)
        col = lax.broadcasted_iota(jnp.int32, shape, 1)
        own = times(tail, (row == at[1] * size + col).astype(f32).astype(bf))
        for i in range(first, last):
            gains[i][...] = own[i, :]


def shards(
    layer_input,
    out_cotangent,
    block_pairs,
    w_query,
    w_key,
    w_value,
    w_output,
    w_gate,
    w_up,
    w_down,
    input_gain,
    attnpost_gain,
    ffnpre_gain,
    ffnpost_gain,
    query_gain,
    key_gain,
):
    S, C = Axis("shard"), Axis("ctx")
    seqs, span, width = layer_input.shape
    rows = seqs * span
    members, count = C.size, S.size
    twin = C.rank % 2
    pq, pk, po, pf = w_query.shape[1], w_key.shape[1], w_output.shape[0], w_down.shape[0]
    hd = query_gain.shape[0] * count
    hq = pq * count
    heads = hq // hd
    scale = hd ** (-0.5)
    where = jnp.stack(S.sources() + [twin]).astype(jnp.int32)
    members_from = jnp.stack(C.sources()).astype(jnp.int32)
    x = layer_input.reshape(rows, width)
    cot = out_cotangent.reshape(rows, width)

    small = [input_gain, attnpost_gain, ffnpre_gain, ffnpost_gain, query_gain, key_gain]

    def placed(same):
        size = same[0].shape[0]
        at = jnp.arange(width)[None, :] == S.rank * size + jnp.arange(size)[:, None]
        return times(jnp.stack(same), at.astype(bf)).astype(bf)

    gain_rows = jnp.concatenate([placed(small[:4]), placed(small[4:])], axis=0)
    gain_rows = jnp.pad(gain_rows, ((0, 8 - len(small)), (0, 0)))

    whole = jnp.concatenate([w_query.T, w_key.T, w_value.T, w_output], axis=0)
    piece = whole.shape[0] // 2
    own = jnp.where(twin == 0, whole[:piece], whole[piece:])
    first = jnp.concatenate([own, gain_rows], axis=0)
    mine = S.gather(first)
    other = [C.send(m, 0, 1) for m in mine]

    pc = pf // members

    def part_of(w):
        return lax.dynamic_slice_in_dim(w, C.rank * pc, pc, 0)

    ffn = jnp.concatenate([part_of(w_gate.T), part_of(w_up.T), part_of(w_down)], axis=0)
    chunks = S.gather(after(ffn, *mine[2::2]))

    places = seq_positions(block_pairs, span // 2)
    kpos = jnp.concatenate(
        [lax.dynamic_index_in_dim(places, o, 1, keepdims=False) for o in C.sources()], axis=1
    )
    own_pos = lax.dynamic_index_in_dim(places, C.rank, 1, keepdims=False).reshape(rows)
    cosine, sine = rope_tables(own_pos, hd)
    qpos = own_pos[:, None]
    key_at = jnp.stack([twin, S.rank]).astype(jnp.int32)
    x, qpos, kpos, members_from, key_at = lax.optimization_barrier(
        (x, qpos, kpos, members_from, key_at)
    )

    wq, wk, wv, gains, nin, qraw, kraw, qrot, kv = call(
        functools.partial(qkv_kernel, count, heads),
        [
            ((hq, width), bf),
            ((hd, width), bf),
            ((hd, width), bf),
            ((8, width), f32),
            ((rows, width), bf),
            ((rows, hq), f32),
            ((rows, hd), f32),
            ((rows, hq), bf),
            ((rows, 2 * hd), bf),
        ],
        (where, x, cosine, sine, *mine, *other),
        scalars=1,
    )
    kvs = C.gather(kv)
    (wo,) = call(
        functools.partial(output_weight_kernel, count, pq + 2 * pk),
        [((hq, width), bf)],
        (where, *mine, *other),
        scalars=1,
    )
    length = members * span
    att, probs, kall, proj, resid, nmid = call(
        functools.partial(attend_kernel, seqs, heads, scale),
        [
            ((rows, hq), bf),
            ((seqs * heads * span, length), f32),
            ((seqs * length, 2 * hd), bf),
            ((rows, width), f32),
            ((rows, width), f32),
            ((rows, width), bf),
        ],
        (qpos, kpos, qrot, x, wo, gains, *kvs),
    )
    hid = count * pc
    wg, wu, wd, nm, gate, up, hidden, keep, give = call(
        functools.partial(ffn_kernel, count, members),
        [
            ((hid, width), bf),
            ((hid, width), bf),
            ((hid, width), bf),
            ((members * rows, width), bf),
            ((members * rows, hid), bf),
            ((members * rows, hid), bf),
            ((members * rows, hid), bf),
            ((C.outer * rows, width), f32),
            ((C.outer * rows, width), bf),
        ],
        (*chunks, *C.gather(nmid)),
    )

    def home(keep, give):
        gave = C.send(give, 0, 1)
        far = []
        for a in range(1, C.outer):
            at = slice(a * rows, (a + 1) * rows)
            part = (keep[at] + gave[at].astype(f32)).astype(bf)
            far.append(C.send(part, C.outer - a, 0))
        return gave, far

    gave, far = home(keep, give)
    layer_output, d_ffn, dg_po = call(
        ffn_end_kernel,
        [((rows, width), bf), ((rows, width), bf), ((1, width), f32)],
        (keep, gave, resid, cot, gains, *far),
    )
    dall, dgate, dup, keep, give = call(
        functools.partial(ffn_back_kernel, members),
        [
            ((members * rows, width), bf),
            ((members * rows, hid), bf),
            ((members * rows, hid), bf),
            ((C.outer * rows, width), f32),
            ((C.outer * rows, width), bf),
        ],
        (wg, wu, wd, gate, up, *C.gather(d_ffn)),
    )
    gave, far = home(keep, give)

    def spread(keep, give, each):
        got = S.send(give, 0, 1)
        n = each + keep.shape[0] - S.outer * each
        parts = call(
            functools.partial(far_kernel, S.outer, each),
            [((n, width), f32)] + [((n, width), bf)] * (S.outer - 1),
            (keep, got),
        )
        return [parts[0]] + [S.send(parts[a], S.outer - a, 0) for a in range(1, S.outer)]

    def summed(terms):
        total = terms[0].astype(f32)
        for term in terms[1:]:
            total = total + term.astype(f32)
        return total.astype(bf)

    fkeep, fgive = call(
        functools.partial(ffn_grad_kernel, count),
        [((S.outer * 3 * pc, width), bf), ((S.outer * 3 * pc, width), bf)],
        (nm, dall, dgate, dup, hidden),
    )
    f_terms = spread(fkeep, fgive, 3 * pc)

    d_resid, d_proj, dqrot, kkeep, kgive, dg_pf, dg_pa = call(
        functools.partial(attend_back_kernel, seqs, heads, scale),
        [
            ((rows, width), f32),
            ((rows, width), bf),
            ((rows, hq), f32),
            ((C.outer * rows, 2 * hd), f32),
            ((C.outer * rows, 2 * hd), bf),
            ((1, width), f32),
            ((1, width), f32),
        ],
        (keep, gave, resid, proj, cot, gains, wo, *far, probs, kall, qrot),
        scratch=[pltpu.VMEM((length, 2 * hd), f32)],
    )
    kgave, kfar = home(kkeep, kgive)

    def begin(keep, give, each):
        got = C.send(give, 0, 1)
        half = S.outer * each
        n = keep.shape[0] - half
        keep, give = call(
            functools.partial(near_kernel, half), [((n, width), f32), ((n, width), bf)], (keep, got)
        )
        return spread(keep, give, each)

    def finish(terms):
        part = summed(terms)
        far = [C.send(part, a, 0) for a in range(1, C.outer)]
        total = summed([part] + far)
        return total, C.send(total, 0, 1)

    each_q, each_k = (pq + po) // 2, pk
    dq, dg_q, keep, give = call(
        functools.partial(query_back_kernel, count, heads),
        [
            ((rows, hq), bf),
            ((1, hd), f32),
            ((count * each_q, width), bf),
            ((count * each_q, width), bf),
        ],
        (where, dqrot, qraw, gains, cosine, sine, nin, att, d_proj),
        scalars=1,
        scratch=[pltpu.VMEM((hq, width), f32), pltpu.VMEM((hq, width), f32)],
    )
    q_got = C.send(give, 0, 1)
    each_q //= C.outer
    q_own, *q_gives = call(
        functools.partial(part_kernel, C.outer, count),
        [((count * each_q, width), f32)] + [((count * each_q, width), bf)] * (C.outer - 1),
        ((C.rank // 2).astype(jnp.int32)[None], keep, q_got),
        scalars=1,
    )
    for a, give in enumerate(q_gives):
        q_own = q_own + C.send(give, a + 1, 0).astype(f32)
    half = S.outer * each_q
    q_terms = spread(q_own[:half], q_own[half:].astype(bf), each_q)
    input_grad, keep, give = call(
        functools.partial(key_back_kernel, count),
        [
            ((rows, width), f32),
            ((count * each_k + 8, width), f32),
            ((count * each_k + 8, width), bf),
        ],
        (
            where,
            kkeep,
            kgave,
            kraw,
            gains,
            cosine,
            sine,
            nin,
            dq,
            wq,
            wk,
            wv,
            x,
            d_resid,
            dg_po,
            dg_pf,
            dg_pa,
            dg_q,
            *kfar,
        ),
        scalars=1,
        scratch=[pltpu.VMEM((hd, width), f32), pltpu.VMEM((hd, width), f32)],
    )
    k_terms = begin(keep, give, each_k)
    all_q = C.gather(summed(q_terms))
    total_k = finish(k_terms)

    out_gate, out_up, out_down = call(
        functools.partial(ffn_out_kernel, members),
        [((width, pf), f32), ((width, pf), f32), ((pf, width), f32)],
        (members_from, *C.gather(summed(f_terms))),
        scalars=1,
        scratch=[pltpu.VMEM((pf, width), f32)],
    )
    out_query, out_output = call(
        functools.partial(query_out_kernel, (pq, po)),
        [((width, pq), f32), ((po, width), f32)],
        (members_from, *all_q),
        scalars=1,
        scratch=[pltpu.VMEM((pq + po, width), f32)],
    )
    out_key, out_value, *sums = call(
        functools.partial(key_out_kernel, (pk, pk)),
        [((pk, width), f32), ((pk, width), f32)] + [(g.shape, f32) for g in small],
        (key_at, *total_k),
        scalars=1,
    )
    out_key, out_value = out_key.T, out_value.T
    return (
        layer_output.reshape(seqs, span, width),
        input_grad.reshape(seqs, span, width),
        out_query,
        out_key,
        out_value,
        out_output,
        out_gate,
        out_up,
        out_down,
        *sums,
    )


def solution(mesh):
    lead2 = P("shard", "ctx", None)
    cols = P(None, "shard")
    lead = P("shard", None)
    gain = P("shard")
    return jax.shard_map(
        shards,
        mesh=mesh,
        in_specs=(lead2, lead2, lead, cols, cols, cols, lead, cols, cols, lead) + (gain,) * 6,
        out_specs=(lead2, lead2, cols, cols, cols, lead, cols, cols, lead) + (gain,) * 6,
        check_vma=False,
    )
```
